512 devices in a mesh: len: 64 (over x, z, core), wid: 8 (over y).
Axes of the slice: x: 4, y: 8, z: 8, core: 2. Of those that a mesh axis runs over, the one named last changes fastest.
Arguments:
- flow_state: float32 [3, 512, 16, 2048], P(None, 'len', None, 'wid'), may hold values from -0.5 to 2
- courant: float32 [512, 16, 2048], P('len', None, 'wid'), as said below
- inflow: float32 [3, 16, 2048], P(None, None, 'wid'), may hold values from -6 to 6
- height_ops: float32 [8, 16, 16], replicated, may hold values from -1.5 to 1.5
- metric_index: int32 [128], P('len'), may hold values from 0 to 7
Outputs:
- new_state: float32 [3, 512, 16, 2048], P(None, 'len', None, 'wid')
- tendency: float32 [3, 512, 16, 2048], P(None, 'len', None, 'wid')
The draws below stay inside these ranges and needn't reach their ends.
Inputs may be any that keep to these rules, and one draw needn't show every extreme that they name: courant is positive.
All inputs are finite; a program needn't handle non-finite values.
Results may differ from the reference program's by a relative error of at most 0.0003.
Values sent between devices are 32-bit elements; how exact they have to be, the bound alone decides.
A program may use at most 64 MiB of HBM per device.

```python
import math
import jax
import jax.numpy as jnp
from jax import lax

HEIGHT_CELLS = 16
GROUP = 4
NMET = 8
LENGTH_CELLS = 512
WIDTH_CELLS = 2048


def draw_courant(key, part):
    key_for_row, key_for_cell, key_for_spot, key_surge = jax.random.split(key, 4)
    exponent = jax.random.uniform(key_for_row, (1, HEIGHT_CELLS, WIDTH_CELLS), jnp.float32, -2.0, 1.5)
    row_fraction = LENGTH_CELLS * jnp.exp(exponent * math.log(10.0))
    random_shift = jnp.exp(jax.random.uniform(key_for_cell, (LENGTH_CELLS, HEIGHT_CELLS, WIDTH_CELLS), jnp.float32, -math.log(2.0), math.log(2.0)))
    surge_spots = jax.random.randint(key_for_spot, (4,), 0, LENGTH_CELLS)
    cell_location = jnp.arange(LENGTH_CELLS, dtype=jnp.int32)
    inside_surge = jnp.any(cell_location[:, None] == surge_spots[None, :], axis=1)[:, None, None]
    surge_rate = jax.random.uniform(key_surge, (LENGTH_CELLS, HEIGHT_CELLS, WIDTH_CELLS), jnp.float32, 1.0, 4.0)
    return jnp.where(inside_surge, surge_rate, jnp.maximum(row_fraction * random_shift, 1.0))


def touch_ends(result, rng, least, top_value):
    longest = result.shape.index(max(result.shape))
    spots = []
    for shift in (0, 1):
        where = [jax.random.randint(jax.random.fold_in(rng, axis), (), 0, length) for axis, length in enumerate(result.shape)]
        where[longest] = (where[longest] + shift) % result.shape[longest]
        spots.append(tuple(where))
    return result.at[spots[0]].set(least).at[spots[1]].set(top_value)


def shard_levels(own_key, extent, pieces, low, high):
    factor_of, own = 1.0, jax.random.fold_in(own_key, 6)
    for position, shards_of in pieces:
        steps = jnp.exp(jax.random.uniform(jax.random.fold_in(own, position), (shards_of,), jnp.float32, low / len(pieces), high / len(pieces)))
        factor_of = factor_of * jnp.repeat(steps, extent[position] // shards_of).reshape([-1 if axis == position else 1 for axis in range(len(extent))])
    return factor_of


def centred(rng, extent, deviation, limit, shards=(), kind=jnp.bfloat16):
    drawn = deviation * jax.random.normal(rng, extent, jnp.float32)
    if shards:
        drawn = drawn * shard_levels(rng, extent, shards, -0.22, 0.18)
    return jnp.clip(drawn, -limit, limit).astype(kind)


def setup_inputs(seed: int = 0) -> dict:
    arg_keys = jax.random.split(jax.random.key(seed), 6)
    return {
        "flow_state": jnp.clip(-0.5 + 2.5 * jax.random.uniform(arg_keys[0], (3, LENGTH_CELLS, HEIGHT_CELLS, WIDTH_CELLS), jnp.float32) ** shard_levels(arg_keys[0], (3, LENGTH_CELLS, HEIGHT_CELLS, WIDTH_CELLS), ((1, 64), (3, 8)), -0.2, 0.2), -0.5, 2.0),
        "courant": draw_courant(jax.random.fold_in(arg_keys[5], 71), 0),
        "inflow": centred(arg_keys[2], (3, HEIGHT_CELLS, WIDTH_CELLS), 1.0, 6.0, ((2, 8),), jnp.float32),
        "height_ops": centred(arg_keys[3], (NMET, HEIGHT_CELLS, HEIGHT_CELLS), HEIGHT_CELLS ** -0.5, 1.5, (), jnp.float32),
        "metric_index": touch_ends(jax.random.randint(arg_keys[4], (LENGTH_CELLS // GROUP,), 0, NMET), jax.random.fold_in(arg_keys[4], 1), 0, NMET - 1).astype(jnp.int32),
    }


def width_slopes(fields):
    padded = jnp.pad(fields, ((0, 0), (0, 0), (0, 0), (3, 3)))
    ncells = fields.shape[3]
    summed = jnp.zeros(fields.shape, jnp.float32)
    for offset, factor in ((1, 45.0 / 60.0), (2, -9.0 / 60.0), (3, 1.0 / 60.0)):
        upper = padded[..., 3 + offset:3 + offset + ncells]
        lower = padded[..., 3 - offset:3 - offset + ncells]
        summed = summed + factor * (upper - lower)
    return summed


def reference(flow_state, courant, inflow, height_ops, metric_index):
    slopes = width_slopes(flow_state)
    cell_ops = height_ops[jnp.repeat(metric_index, GROUP)]
    vertical = jnp.einsum("xab,fxby->fxay", cell_ops, flow_state, precision=lax.Precision.HIGHEST)
    tendency = -flow_state[1:2] * slopes + vertical
    target = flow_state + 0.25 * tendency
    keep_rate = courant / (1.0 + courant)
    take_rate = 1.0 / (1.0 + courant)

    def advance(carried, inputs):
        keep_now, take_now, target_now = inputs
        updated = keep_now * carried + take_now * target_now
        return updated, updated

    last_state, swept = lax.scan(advance, inflow, (keep_rate, take_rate, jnp.moveaxis(target, 1, 0)))
    return jnp.moveaxis(swept, 0, 1), tendency
```

```python
import functools

import jax
import jax.numpy as jnp
from jax import lax
from jax.experimental import pallas as pl
from jax.experimental.pallas import tpu as pltpu
from jax.sharding import PartitionSpec as P

STEP = 0.25
LANE = 128
SUB = 8
MESH = pl.DeviceIdType.MESH


def split_bf16(value):
    high = value.astype(jnp.bfloat16)
    return high, (value - high.astype(jnp.float32)).astype(jnp.bfloat16)


def sweep_kernel(
    inner, outer, nwid, groups,
    flow_hbm, cour_hbm, inflow_hbm, ops_hbm, metric_hbm,
    new_ref, tend_ref,
    flow, cour, infl, ops, metric, prod, halo_out, halo_in,
    send1, recv1, send2, recv2, send3, recv3,
    in_sem, halo_send, halo_recv, ex_send, ex_recv,
):
    fields, nx, nz, ny = flow.shape
    nh, nl = nz // SUB, ny // LANE
    per = nz // inner
    chunk = per * SUB
    me = lax.axis_index("len")
    wid = lax.axis_index("wid")
    mine = lax.rem(me, inner)
    block = lax.div(me, inner)
    right, left = lax.rem(wid + 1, nwid), lax.rem(wid + nwid - 1, nwid)

    loads = [
        pltpu.make_async_copy(src, dst, in_sem.at[i])
        for i, (src, dst) in enumerate(
            ((flow_hbm, flow), (cour_hbm, cour), (inflow_hbm, infl), (ops_hbm, ops), (metric_hbm, metric))
        )
    ]
    for load in loads:
        load.start()

    def group_peer(j):
        return lax.rem(mine + j, inner)

    def block_peer(j):
        return lax.rem(block + j, outer)

    barrier = pltpu.get_barrier_semaphore()
    pl.semaphore_signal(barrier, inc=1, device_id=(me, left), device_id_type=MESH)
    pl.semaphore_signal(barrier, inc=1, device_id=(me, right), device_id_type=MESH)
    for j in range(1, inner):
        pl.semaphore_signal(
            barrier, inc=1, device_id=(block * inner + group_peer(j), wid), device_id_type=MESH
        )
    for j in range(1, outer):
        pl.semaphore_signal(
            barrier, inc=1, device_id=(block_peer(j) * inner + mine, wid), device_id_type=MESH
        )

    loads[4].wait()
    loads[3].wait()
    rows = nx * nz
    tiles = []
    for g in range(groups):
        one = ops[metric[g]]
        tiles.append(jnp.concatenate([one] * nx, axis=1))
    row_cell = lax.broadcasted_iota(jnp.int32, (nz, rows), 1) // nz
    diag = jnp.concatenate(
        [jnp.where(row_cell == i, tiles[i * groups // nx], 0.0) for i in range(nx)], axis=0
    )
    diag_high, diag_low = split_bf16(diag)

    loads[1].wait()
    take = []
    keep = []
    for i in range(nx):
        c = cour[i]
        t = 1.0 / (1.0 + c)
        take.append(t)
        keep.append(jnp.where(c < 1.0, c * t, 1.0 - t))
        prod[i] = keep[i] if i == 0 else keep[i] * prod[i - 1]

    loads[2].wait()
    row = lax.broadcasted_iota(jnp.int32, (SUB, LANE), 0)
    lane = lax.broadcasted_iota(jnp.int32, (SUB, LANE), 1)
    slot, spot = lane // 4, lane % 4
    height = lax.broadcasted_iota(jnp.int32, (nz, LANE), 0)
    starts = []
    for p in range(per):
        tile = jnp.zeros((SUB, LANE), jnp.float32)
        for f in range(fields):
            for l in range(nl):
                line = jnp.where(height == mine * per + p, infl[f, :, l * LANE:(l + 1) * LANE], 0.0)
                line = jnp.sum(line, axis=0, keepdims=True)
                tile = jnp.where(row == (1 + f) * nl + l, jnp.broadcast_to(line, (SUB, LANE)), tile)
        starts.append(tile)

    loads[0].wait()
    nrow = fields * nx * nh
    slots = LANE // 4
    npack = pl.cdiv(nrow, slots)

    def where_is(r):
        f, i, h = r // (nx * nh), (r // nh) % nx, r % nh
        return f, i, slice(h * SUB, (h + 1) * SUB)

    packed = []
    for v in range(npack):
        low = jnp.zeros((SUB, LANE), jnp.float32)
        high = low
        for s in range(min(slots, nrow - v * slots)):
            f, i, z = where_is(v * slots + s)
            here = slot == s
            first, last = flow[f, i, z, :LANE], flow[f, i, z, ny - LANE:]
            low = jnp.where(here, pltpu.roll(first, 4 * s, 1) if s else first, low)
            high = jnp.where(here, pltpu.roll(last, (4 * s + 3) % LANE, 1), high)
        low = jnp.where(spot < 3, low, 0.0)
        high = jnp.where(spot < 3, high, 0.0)
        packed.append((low, high))
        halo_out[0, v] = low
        halo_out[1, v] = high

    pl.semaphore_wait(barrier, 2 + (inner - 1) + (outer - 1))
    halos = [
        pltpu.make_async_remote_copy(
            src_ref=halo_out.at[side],
            dst_ref=halo_in.at[side],
            send_sem=halo_send.at[side],
            recv_sem=halo_recv.at[side],
            device_id=(me, to),
            device_id_type=MESH,
        )
        for side, to in ((0, left), (1, right))
    ]
    for halo in halos:
        halo.start()

    for f in range(fields):
        q = flow[f].reshape(rows, ny)
        q_high, q_low = split_bf16(q)
        vertical = jnp.dot(diag_high, q_high, preferred_element_type=jnp.float32)
        vertical += jnp.dot(diag_low, q_high, preferred_element_type=jnp.float32)
        vertical += jnp.dot(diag_high, q_low, preferred_element_type=jnp.float32)
        for i in range(nx):
            q = flow[f, i]
            slopes = jnp.zeros((nz, ny), jnp.float32)
            for offset, factor in ((1, 45.0 / 60.0), (2, -9.0 / 60.0), (3, 1.0 / 60.0)):
                slopes += factor * (pltpu.roll(q, ny - offset, 1) - pltpu.roll(q, offset, 1))
            tend_ref[f, i] = vertical[i * nz:(i + 1) * nz] - flow[1, i] * slopes

    for halo in halos:
        halo.wait_recv()
    for v in range(npack):
        low, high = packed[v]
        before = jnp.where(wid == 0, 0.0, halo_in[1, v]) - high
        after = jnp.where(wid == nwid - 1, 0.0, halo_in[0, v]) - low
        fix_low = (
            (-1.0 / 60.0) * before
            + jnp.where(spot < 2, 9.0 / 60.0, 0.0) * pltpu.roll(before, LANE - 1, 1)
            + jnp.where(spot < 1, -45.0 / 60.0, 0.0) * pltpu.roll(before, LANE - 2, 1)
        )
        fix_high = (
            (1.0 / 60.0) * after
            + jnp.where(spot >= 1, -9.0 / 60.0, 0.0) * pltpu.roll(after, 1, 1)
            + jnp.where(spot >= 2, 45.0 / 60.0, 0.0) * pltpu.roll(after, 2, 1)
        )
        for s in range(min(slots, nrow - v * slots)):
            f, i, z = where_is(v * slots + s)
            fix = pltpu.roll(fix_low, LANE - 4 * s, 1) if s else fix_low
            fix = jnp.where(lane < 3, fix, 0.0)
            tend_ref[f, i, z, :LANE] -= flow[1, i, z, :LANE] * fix
            fix = pltpu.roll(fix_high, (2 * LANE - 3 - 4 * s) % LANE, 1)
            fix = jnp.where(lane >= LANE - 3, fix, 0.0)
            tend_ref[f, i, z, ny - LANE:] -= flow[1, i, z, ny - LANE:] * fix

    for f in range(fields):
        state = None
        for i in range(nx):
            c = cour[i]
            t = 1.0 / (1.0 + c)
            k = jnp.where(c < 1.0, c * t, 1.0 - t)
            gain = t * (flow[f, i] + STEP * tend_ref[f, i])
            state = gain if state is None else k * state + gain
            new_ref[f, i] = state

    def scatter(value, v):
        for h in range(nh):
            for l in range(nl):
                send1[pl.ds(h * SUB * SUB + v * nl + l, SUB, stride=SUB), :] = value[
                    h * SUB:(h + 1) * SUB, l * LANE:(l + 1) * LANE
                ]

    scatter(prod[nx - 1], 0)
    for f in range(fields):
        scatter(new_ref[f, nx - 1], 1 + f)

    def part(ref, k):
        return ref.at[pl.ds(pl.multiple_of(k * chunk, SUB), chunk), :]

    def exchange(source_of, into, at, peers, phase):
        for peer, device in peers:
            pltpu.make_async_remote_copy(
                src_ref=source_of(peer),
                dst_ref=part(into, at),
                send_sem=ex_send.at[phase],
                recv_sem=ex_recv.at[phase],
                device_id=(device, wid),
                device_id_type=MESH,
            ).start()

    def total(ref, count, phase):
        span = ref.at[pl.ds(0, count * chunk), :]
        return pltpu.make_async_remote_copy(
            src_ref=span,
            dst_ref=span,
            send_sem=ex_send.at[phase],
            recv_sem=ex_recv.at[phase],
            device_id=(me, right),
            device_id_type=MESH,
        )

    group = [(group_peer(j), block * inner + group_peer(j)) for j in range(1, inner)]
    blocks = [(block_peer(j), block_peer(j) * inner + mine) for j in range(1, outer)]

    exchange(lambda k: part(send1, k), recv1, mine, group, 0)
    own = pl.ds(pl.multiple_of(mine * chunk, SUB), chunk)
    recv1[own, :] = send1[own, :]
    total(recv1, inner - 1, 0).wait_recv()

    def load_map(ref, at):
        tile = ref[at:at + SUB, :]
        decay = jnp.broadcast_to(tile[0:1], (SUB, LANE))
        for l in range(1, nl):
            decay = jnp.where(row % nl == l, jnp.broadcast_to(tile[l:l + 1], (SUB, LANE)), decay)
        return decay, tile

    prefix = []
    for p in range(per):
        decay, state = jnp.ones((SUB, LANE), jnp.float32), jnp.zeros((SUB, LANE), jnp.float32)
        line = []
        for k in range(inner):
            line.append((decay, state))
            d, s = load_map(recv1, k * chunk + p * SUB)
            decay, state = d * decay, d * state + s
        prefix.append(line)
        send2[p * SUB:(p + 1) * SUB, :] = jnp.where(row < nl, decay, state)

    if outer > 1:
        exchange(lambda k: send2, recv2, block, blocks, 1)
        own = pl.ds(pl.multiple_of(block * chunk, SUB), chunk)
        recv2[own, :] = send2[...]
        total(recv2, outer - 1, 1).wait_recv()
    for p in range(per):
        entry = starts[p]
        for b in range(outer - 1):
            d, s = load_map(recv2, b * chunk + p * SUB)
            entry = jnp.where(b < block, d * entry + s, entry)
        for k in range(inner):
            d, s = prefix[p][k]
            send3[k * chunk + p * SUB:k * chunk + (p + 1) * SUB, :] = d * entry + s

    exchange(lambda k: part(send3, k), recv3, mine, group, 2)
    own = pl.ds(pl.multiple_of(mine * chunk, SUB), chunk)
    recv3[own, :] = send3[own, :]
    total(recv3, inner - 1, 2).wait_recv()
    for f in range(fields):
        for h in range(nh):
            for l in range(nl):
                enter = recv3[pl.ds(h * SUB * SUB + (1 + f) * nl + l, SUB, stride=SUB), :]
                z, y = slice(h * SUB, (h + 1) * SUB), slice(l * LANE, (l + 1) * LANE)
                for i in range(nx):
                    new_ref[f, i, z, y] += prod[i, z, y] * enter

    for halo in halos:
        halo.wait_send()
    total(send1, inner - 1, 0).wait_send()
    if outer > 1:
        total(recv2, outer - 1, 1).wait_send()
    total(send3, inner - 1, 2).wait_send()


def shards(inner, flow_state, courant, inflow, height_ops, metric_index):
    fields, nx, nz, ny = flow_state.shape
    count = lax.axis_size("len")
    nwid = lax.axis_size("wid")
    outer = count // inner
    chunk = nz // inner * SUB
    out = jax.ShapeDtypeStruct(flow_state.shape, jnp.float32)
    anywhere = pl.BlockSpec(memory_space=pl.ANY)
    nrow = fields * nx * (nz // SUB)
    npack = pl.cdiv(nrow, LANE // 4)
    f32 = jnp.float32
    dma = pltpu.SemaphoreType.DMA
    return pl.pallas_call(
        functools.partial(sweep_kernel, inner, outer, nwid, metric_index.shape[0]),
        out_shape=(out, out),
        in_specs=[anywhere] * 5,
        out_specs=(pl.BlockSpec(memory_space=pltpu.VMEM),) * 2,
        scratch_shapes=[
            pltpu.VMEM(flow_state.shape, f32),
            pltpu.VMEM(courant.shape, f32),
            pltpu.VMEM(inflow.shape, f32),
            pltpu.VMEM(height_ops.shape, f32),
            pltpu.SMEM(metric_index.shape, jnp.int32),
            pltpu.VMEM(courant.shape, f32),
            pltpu.VMEM((2, npack, SUB, LANE), f32),
            pltpu.VMEM((2, npack, SUB, LANE), f32),
            pltpu.VMEM((inner * chunk, LANE), f32),
            pltpu.VMEM((inner * chunk, LANE), f32),
            pltpu.VMEM((chunk, LANE), f32),
            pltpu.VMEM((outer * chunk, LANE), f32),
            pltpu.VMEM((inner * chunk, LANE), f32),
            pltpu.VMEM((inner * chunk, LANE), f32),
            dma((5,)),
            dma((2,)),
            dma((2,)),
            dma((3,)),
            dma((3,)),
        ],
        compiler_params=pltpu.CompilerParams(collective_id=0, has_side_effects=True),
        name="sweep",
    )(flow_state, courant, inflow, height_ops, metric_index)


def solution(mesh, inner=16):
    placed = (
        P(None, "len", None, "wid"),
        P("len", None, "wid"),
        P(None, None, "wid"),
        P(),
        P("len"),
    )
    return jax.shard_map(
        functools.partial(shards, inner),
        mesh=mesh,
        in_specs=placed,
        out_specs=(P(None, "len", None, "wid"), P(None, "len", None, "wid")),
        check_vma=False,
    )
```

```python
import functools

import jax
import jax.numpy as jnp
from jax import lax
from jax.experimental import pallas as pl
from jax.experimental.pallas import tpu as pltpu
from jax.sharding import PartitionSpec as P

STEP = 0.25
LANE = 128
SUB = 8
MESH = pl.DeviceIdType.MESH


def split_bf16(value):
    high = value.astype(jnp.bfloat16)
    return high, (value - high.astype(jnp.float32)).astype(jnp.bfloat16)


def sweep_kernel(
    inner, outer, nwid, groups,
    flow_hbm, cour_hbm, inflow_hbm, ops_hbm, metric_hbm,
    new_ref, tend_ref,
    flow, cour, infl, ops, metric, prod, halo_out, halo_in,
    send1, recv1, send2, recv2, send3, recv3,
    in_sem, halo_send, halo_recv, ex_send, ex_recv,
):
    fields, nx, nz, ny = flow.shape
    nh, nl = nz // SUB, ny // LANE
    owners = inner // 2
    shift = inner * 3 // 4
    per = nz // owners
    chunk = per * SUB
    me = lax.axis_index("len")
    wid = lax.axis_index("wid")
    mine = lax.rem(me, inner)
    block = lax.div(me, inner)
    right, left = lax.rem(wid + 1, nwid), lax.rem(wid + nwid - 1, nwid)

    loads = [
        pltpu.make_async_copy(src, dst, in_sem.at[i])
        for i, (src, dst) in enumerate(
            ((flow_hbm, flow), (cour_hbm, cour), (inflow_hbm, infl), (ops_hbm, ops), (metric_hbm, metric))
        )
    ]
    for load in loads:
        load.start()

    rank = lax.rem(mine + (inner - shift), inner)
    owner = rank < owners
    owner_order = list(range(owners // 2, owners))[::-1] + list(range(owners // 2))

    barrier = pltpu.get_barrier_semaphore()

    def greet(to, across):
        pl.semaphore_signal(barrier, inc=1, device_id=(to, across), device_id_type=MESH)

    greet(me, left)
    greet(me, right)
    for k in range(inner):
        met = mine != k
        if (k - shift) % inner >= owners:
            met = jnp.logical_and(met, owner)

        @pl.when(met)
        def _():
            greet(block * inner + k, wid)

    @pl.when(owner)
    def _():
        for j in range(1, outer):
            greet(lax.rem(block + j, outer) * inner + mine, wid)

    loads[4].wait()
    loads[3].wait()
    rows = nx * nz
    tiles = []
    for g in range(groups):
        one = ops[metric[g]]
        tiles.append(jnp.concatenate([one] * nx, axis=1))
    row_cell = lax.broadcasted_iota(jnp.int32, (nz, rows), 1) // nz
    diag = jnp.concatenate(
        [jnp.where(row_cell == i, tiles[i * groups // nx], 0.0) for i in range(nx)], axis=0
    )
    diag_high, diag_low = split_bf16(diag)

    loads[1].wait()
    take = []
    keep = []
    for i in range(nx):
        c = cour[i]
        t = 1.0 / (1.0 + c)
        take.append(t)
        keep.append(jnp.where(c < 1.0, c * t, 1.0 - t))
        prod[i] = keep[i] if i == 0 else keep[i] * prod[i - 1]

    loads[2].wait()
    row = lax.broadcasted_iota(jnp.int32, (SUB, LANE), 0)
    lane = lax.broadcasted_iota(jnp.int32, (SUB, LANE), 1)
    slot, spot = lane // 4, lane % 4
    height = lax.broadcasted_iota(jnp.int32, (nz, LANE), 0)
    starts = []
    for p in range(per):
        tile = jnp.zeros((SUB, LANE), jnp.float32)
        for f in range(fields):
            for l in range(nl):
                line = jnp.where(height == rank * per + p, infl[f, :, l * LANE:(l + 1) * LANE], 0.0)
                line = jnp.sum(line, axis=0, keepdims=True)
                tile = jnp.where(row == (1 + f) * nl + l, jnp.broadcast_to(line, (SUB, LANE)), tile)
        starts.append(tile)

    loads[0].wait()
    nrow = fields * nx * nh
    slots = LANE // 4
    npack = pl.cdiv(nrow, slots)

    def where_is(r):
        f, i, h = r // (nx * nh), (r // nh) % nx, r % nh
        return f, i, slice(h * SUB, (h + 1) * SUB)

    packed = []
    for v in range(npack):
        low = jnp.zeros((SUB, LANE), jnp.float32)
        high = low
        for s in range(min(slots, nrow - v * slots)):
            f, i, z = where_is(v * slots + s)
            here = slot == s
            first, last = flow[f, i, z, :LANE], flow[f, i, z, ny - LANE:]
            low = jnp.where(here, pltpu.roll(first, 4 * s, 1) if s else first, low)
            high = jnp.where(here, pltpu.roll(last, (4 * s + 3) % LANE, 1), high)
        low = jnp.where(spot < 3, low, 0.0)
        high = jnp.where(spot < 3, high, 0.0)
        packed.append((low, high))
        halo_out[0, v] = low
        halo_out[1, v] = high

    @pl.when(owner)
    def _():
        pl.semaphore_wait(barrier, 2 + (inner - 1) + (outer - 1))

    @pl.when(jnp.logical_not(owner))
    def _():
        pl.semaphore_wait(barrier, 2 + owners)

    halos = [
        pltpu.make_async_remote_copy(
            src_ref=halo_out.at[side],
            dst_ref=halo_in.at[side],
            send_sem=halo_send.at[side],
            recv_sem=halo_recv.at[side],
            device_id=(me, to),
            device_id_type=MESH,
        )
        for side, to in ((0, left), (1, right))
    ]
    for halo in halos:
        halo.start()

    for f in range(fields):
        q = flow[f].reshape(rows, ny)
        q_high, q_low = split_bf16(q)
        vertical = jnp.dot(diag_high, q_high, preferred_element_type=jnp.float32)
        vertical += jnp.dot(diag_low, q_high, preferred_element_type=jnp.float32)
        vertical += jnp.dot(diag_high, q_low, preferred_element_type=jnp.float32)
        for i in range(nx):
            q = flow[f, i]
            slopes = jnp.zeros((nz, ny), jnp.float32)
            for offset, factor in ((1, 45.0 / 60.0), (2, -9.0 / 60.0), (3, 1.0 / 60.0)):
                slopes += factor * (pltpu.roll(q, ny - offset, 1) - pltpu.roll(q, offset, 1))
            tend_ref[f, i] = vertical[i * nz:(i + 1) * nz] - flow[1, i] * slopes

    for halo in halos:
        halo.wait_recv()
    for v in range(npack):
        low, high = packed[v]
        before = jnp.where(wid == 0, 0.0, halo_in[1, v]) - high
        after = jnp.where(wid == nwid - 1, 0.0, halo_in[0, v]) - low
        fix_low = (
            (-1.0 / 60.0) * before
            + jnp.where(spot < 2, 9.0 / 60.0, 0.0) * pltpu.roll(before, LANE - 1, 1)
            + jnp.where(spot < 1, -45.0 / 60.0, 0.0) * pltpu.roll(before, LANE - 2, 1)
        )
        fix_high = (
            (1.0 / 60.0) * after
            + jnp.where(spot >= 1, -9.0 / 60.0, 0.0) * pltpu.roll(after, 1, 1)
            + jnp.where(spot >= 2, 45.0 / 60.0, 0.0) * pltpu.roll(after, 2, 1)
        )
        for s in range(min(slots, nrow - v * slots)):
            f, i, z = where_is(v * slots + s)
            fix = pltpu.roll(fix_low, LANE - 4 * s, 1) if s else fix_low
            fix = jnp.where(lane < 3, fix, 0.0)
            tend_ref[f, i, z, :LANE] -= flow[1, i, z, :LANE] * fix
            fix = pltpu.roll(fix_high, (2 * LANE - 3 - 4 * s) % LANE, 1)
            fix = jnp.where(lane >= LANE - 3, fix, 0.0)
            tend_ref[f, i, z, ny - LANE:] -= flow[1, i, z, ny - LANE:] * fix

    for f in range(fields):
        state = None
        for i in range(nx):
            c = cour[i]
            t = 1.0 / (1.0 + c)
            k = jnp.where(c < 1.0, c * t, 1.0 - t)
            gain = t * (flow[f, i] + STEP * tend_ref[f, i])
            state = gain if state is None else k * state + gain
            new_ref[f, i] = state

    def scatter(value, v):
        for h in range(nh):
            for l in range(nl):
                send1[pl.ds(h * SUB * SUB + v * nl + l, SUB, stride=SUB), :] = value[
                    h * SUB:(h + 1) * SUB, l * LANE:(l + 1) * LANE
                ]

    scatter(prod[nx - 1], 0)
    for f in range(fields):
        scatter(new_ref[f, nx - 1], 1 + f)

    def remote(source, target, phase, slot, device):
        return pltpu.make_async_remote_copy(
            src_ref=source,
            dst_ref=target,
            send_sem=ex_send.at[phase],
            recv_sem=ex_recv.at[slot],
            device_id=(device, wid),
            device_id_type=MESH,
        )

    def part(ref, k):
        return ref.at[pl.ds(k * chunk if isinstance(k, int) else pl.multiple_of(k * chunk, SUB), chunk), :]

    def total(ref, count, phase):
        span = ref.at[pl.ds(0, count * chunk), :]
        return remote(span, span, phase, phase, me)

    def load_map(ref, at):
        tile = ref[at:at + SUB, :]
        decay = jnp.broadcast_to(tile[0:1], (SUB, LANE))
        for l in range(1, nl):
            decay = jnp.where(row % nl == l, jnp.broadcast_to(tile[l:l + 1], (SUB, LANE)), decay)
        return decay, tile

    for w in owner_order:
        k = (w + shift) % inner

        @pl.when(mine != k)
        def _():
            remote(part(send1, w), part(recv1, mine), 0, 0, block * inner + k).start()

    @pl.when(owner)
    def _():
        own = pl.ds(pl.multiple_of(mine * chunk, SUB), chunk)
        recv1[own, :] = send1[pl.ds(pl.multiple_of(rank * chunk, SUB), chunk), :]
        total(recv1, inner - 1, 0).wait_recv()
        prefix = []
        for p in range(per):
            decay, state = jnp.ones((SUB, LANE), jnp.float32), jnp.zeros((SUB, LANE), jnp.float32)
            line = []
            for k in range(inner):
                line.append((decay, state))
                d, s = load_map(recv1, k * chunk + p * SUB)
                decay, state = d * decay, d * state + s
            prefix.append(line)
            send2[p * SUB:(p + 1) * SUB, :] = jnp.where(row < nl, decay, state)

        for j in range(1, outer):
            @pl.when(block + j < outer)
            def _():
                remote(send2, part(recv2, block), 1, 3 + block, (block + j) * inner + mine).start()

        for b in range(outer - 1):
            @pl.when(b < block)
            def _():
                remote(send2, part(recv2, b), 1, 3 + b, me).wait_recv()

        for p in range(per):
            entry = starts[p]
            for b in range(outer - 1):
                d, s = load_map(recv2, b * chunk + p * SUB)
                entry = jnp.where(b < block, d * entry + s, entry)
            for k in range(inner):
                d, s = prefix[p][k]
                send3[k * chunk + p * SUB:k * chunk + (p + 1) * SUB, :] = d * entry + s

        for k in range(inner):
            @pl.when(mine != k)
            def _():
                remote(part(send3, k), part(recv3, rank), 2, 2, block * inner + k).start()

        own = pl.ds(pl.multiple_of(rank * chunk, SUB), chunk)
        recv3[own, :] = send3[pl.ds(pl.multiple_of(mine * chunk, SUB), chunk), :]
        total(recv3, owners - 1, 2).wait_recv()

    @pl.when(jnp.logical_not(owner))
    def _():
        total(recv3, owners, 2).wait_recv()

    for f in range(fields):
        for h in range(nh):
            for l in range(nl):
                enter = recv3[pl.ds(h * SUB * SUB + (1 + f) * nl + l, SUB, stride=SUB), :]
                z, y = slice(h * SUB, (h + 1) * SUB), slice(l * LANE, (l + 1) * LANE)
                for i in range(nx):
                    new_ref[f, i, z, y] += prod[i, z, y] * enter

    for halo in halos:
        halo.wait_send()

    @pl.when(owner)
    def _():
        total(send1, owners - 1, 0).wait_send()
        for j in range(1, outer):
            @pl.when(block + j < outer)
            def _():
                remote(send2, send2, 1, 1, me).wait_send()
        total(send3, inner - 1, 2).wait_send()

    @pl.when(jnp.logical_not(owner))
    def _():
        total(send1, owners, 0).wait_send()


def store_kernel(new_in, tend_in, new_out, tend_out, sem):
    copies = [
        pltpu.make_async_copy(src, dst, sem.at[i])
        for i, (src, dst) in enumerate(((new_in, new_out), (tend_in, tend_out)))
    ]
    for copy in copies:
        copy.start()
    for copy in copies:
        copy.wait()


def shards(inner, flow_state, courant, inflow, height_ops, metric_index):
    fields, nx, nz, ny = flow_state.shape
    count = lax.axis_size("len")
    nwid = lax.axis_size("wid")
    outer = count // inner
    owners = inner // 2
    chunk = nz // owners * SUB
    out = jax.ShapeDtypeStruct(flow_state.shape, jnp.float32)
    anywhere = pl.BlockSpec(memory_space=pl.ANY)
    nrow = fields * nx * (nz // SUB)
    npack = pl.cdiv(nrow, LANE // 4)
    f32 = jnp.float32
    dma = pltpu.SemaphoreType.DMA
    held = [
        pltpu.with_memory_space_constraint(value, pltpu.HBM)
        for value in (flow_state, courant, inflow, height_ops, metric_index)
    ]
    new_state, tendency = pl.pallas_call(
        functools.partial(sweep_kernel, inner, outer, nwid, metric_index.shape[0]),
        out_shape=(out, out),
        in_specs=[pl.BlockSpec(memory_space=pltpu.HBM)] * 5,
        out_specs=(pl.BlockSpec(memory_space=pltpu.VMEM),) * 2,
        scratch_shapes=[
            pltpu.VMEM(flow_state.shape, f32),
            pltpu.VMEM(courant.shape, f32),
            pltpu.VMEM(inflow.shape, f32),
            pltpu.VMEM(height_ops.shape, f32),
            pltpu.SMEM(metric_index.shape, jnp.int32),
            pltpu.VMEM(courant.shape, f32),
            pltpu.VMEM((2, npack, SUB, LANE), f32),
            pltpu.VMEM((2, npack, SUB, LANE), f32),
            pltpu.VMEM((owners * chunk, LANE), f32),
            pltpu.VMEM((inner * chunk, LANE), f32),
            pltpu.VMEM((chunk, LANE), f32),
            pltpu.VMEM((outer * chunk, LANE), f32),
            pltpu.VMEM((inner * chunk, LANE), f32),
            pltpu.VMEM((owners * chunk, LANE), f32),
            dma((5,)),
            dma((2,)),
            dma((2,)),
            dma((3,)),
            dma((3 + outer,)),
        ],
        compiler_params=pltpu.CompilerParams(
            collective_id=0, has_side_effects=True, vmem_limit_bytes=16 << 20
        ),
        name="sweep",
    )(*held)
    return pl.pallas_call(
        store_kernel,
        out_shape=(out, out),
        in_specs=[anywhere] * 2,
        out_specs=(anywhere, anywhere),
        scratch_shapes=[dma((2,))],
        compiler_params=pltpu.CompilerParams(vmem_limit_bytes=4 << 20),
        name="finish",
    )(new_state, tendency)


def solution(mesh, inner=16):
    placed = (
        P(None, "len", None, "wid"),
        P("len", None, "wid"),
        P(None, None, "wid"),
        P(),
        P("len"),
    )
    return jax.shard_map(
        functools.partial(shards, inner),
        mesh=mesh,
        in_specs=placed,
        out_specs=(P(None, "len", None, "wid"), P(None, "len", None, "wid")),
        check_vma=False,
    )
```

```python
import functools

import jax
import jax.numpy as jnp
from jax import lax
from jax.experimental import pallas as pl
from jax.experimental.pallas import tpu as pltpu
from jax.sharding import PartitionSpec as P

STEP = 0.25
SHIFT = 0
LANE = 128
SUB = 8
MESH = pl.DeviceIdType.MESH


def split_bf16(value):
    high = value.astype(jnp.bfloat16)
    return high, (value - high.astype(jnp.float32)).astype(jnp.bfloat16)


def sweep_kernel(
    inner, outer, deep, nwid, groups,
    flow_hbm, cour_hbm, inflow_hbm, ops_hbm, metric_hbm,
    new_ref, tend_ref,
    flow, cour, infl, ops, metric, prod, keep, gain, halo_out, halo_in,
    send1, recv1, send3, recv3,
    in_sem, halo_send, halo_recv, ex_send, ex_recv,
):
    fields, nx, nz, ny = flow.shape
    nh, nl = nz // SUB, ny // LANE
    count = inner * outer
    owners = deep * outer
    per = nz // owners
    chunk = per * SUB
    half = inner // 2
    me = lax.axis_index("len")
    wid = lax.axis_index("wid")
    mine = lax.rem(me, inner)
    block = lax.div(me, inner)
    right, left = lax.rem(wid + 1, nwid), lax.rem(wid + nwid - 1, nwid)

    loads = [
        pltpu.make_async_copy(src, dst, in_sem.at[i])
        for i, (src, dst) in enumerate(
            ((flow_hbm, flow), (cour_hbm, cour), (inflow_hbm, infl), (ops_hbm, ops), (metric_hbm, metric))
        )
    ]
    for load in loads:
        load.start()

    place = lax.rem(mine + (inner - SHIFT), inner)
    owner = place < deep
    rank = block + outer * place

    def seat(w):
        return (w % outer) * inner + (SHIFT + w // outer) % inner

    barrier = pltpu.get_barrier_semaphore()

    def greet(to, across):
        pl.semaphore_signal(barrier, inc=1, device_id=(to, across), device_id_type=MESH)

    greet(me, left)
    greet(me, right)
    seats = [seat(w) for w in range(owners)]
    for t in seats:
        @pl.when(me != t)
        def _():
            greet(t, wid)

    @pl.when(owner)
    def _():
        for t in range(count):
            if t not in seats:
                greet(t, wid)

    row = lax.broadcasted_iota(jnp.int32, (SUB, LANE), 0)
    lane = lax.broadcasted_iota(jnp.int32, (SUB, LANE), 1)
    slot, spot = lane // 4, lane % 4

    loads[0].wait()
    nrow = fields * nx * nh
    slots = LANE // 4
    npack = pl.cdiv(nrow, slots)

    def where_is(r):
        f, i, h = r // (nx * nh), (r // nh) % nx, r % nh
        return f, i, slice(h * SUB, (h + 1) * SUB)

    packed = []
    for v in range(npack):
        low = jnp.zeros((SUB, LANE), jnp.float32)
        high = low
        for s in range(min(slots, nrow - v * slots)):
            f, i, z = where_is(v * slots + s)
            here = slot == s
            first, last = flow[f, i, z, :LANE], flow[f, i, z, ny - LANE:]
            low = jnp.where(here, pltpu.roll(first, 4 * s, 1) if s else first, low)
            high = jnp.where(here, pltpu.roll(last, (4 * s + 3) % LANE, 1), high)
        low = jnp.where(spot < 3, low, 0.0)
        high = jnp.where(spot < 3, high, 0.0)
        packed.append((low, high))
        halo_out[0, v] = low
        halo_out[1, v] = high

    @pl.when(owner)
    def _():
        pl.semaphore_wait(barrier, 2 + count - 1)

    @pl.when(jnp.logical_not(owner))
    def _():
        pl.semaphore_wait(barrier, 2 + owners)

    halos = [
        pltpu.make_async_remote_copy(
            src_ref=halo_out.at[side],
            dst_ref=halo_in.at[side],
            send_sem=halo_send.at[side],
            recv_sem=halo_recv.at[side],
            device_id=(me, to),
            device_id_type=MESH,
        )
        for side, to in ((0, left), (1, right))
    ]
    for halo in halos:
        halo.start()

    loads[4].wait()
    loads[3].wait()
    rows = nx * nz
    tiles = []
    for g in range(groups):
        one = ops[metric[g]]
        tiles.append(jnp.concatenate([one] * nx, axis=1))
    row_cell = lax.broadcasted_iota(jnp.int32, (nz, rows), 1) // nz
    diag = jnp.concatenate(
        [jnp.where(row_cell == i, tiles[i * groups // nx], 0.0) for i in range(nx)], axis=0
    )
    diag_high, diag_low = split_bf16(diag)

    loads[1].wait()
    for i in range(nx):
        c = cour[i]
        t = 1.0 / (1.0 + c)
        cour[i] = t
        k = jnp.where(c < 1.0, c * t, 1.0 - t)
        keep[i] = k
        gain[i] = STEP * t * flow[1, i]
        prod[i] = k if i == 0 else k * prod[i - 1]

    loads[2].wait()
    height = lax.broadcasted_iota(jnp.int32, (nz, LANE), 0)
    starts = []
    for p in range(per):
        tile = jnp.zeros((SUB, LANE), jnp.float32)
        for f in range(fields):
            for l in range(nl):
                line = jnp.where(height == rank * per + p, infl[f, :, l * LANE:(l + 1) * LANE], 0.0)
                line = jnp.sum(line, axis=0, keepdims=True)
                tile = jnp.where(row == (1 + f) * nl + l, jnp.broadcast_to(line, (SUB, LANE)), tile)
        starts.append(tile)

    for f in range(fields):
        q = flow[f].reshape(rows, ny)
        q_high, q_low = split_bf16(q)
        vertical = jnp.dot(diag_high, q_high, preferred_element_type=jnp.float32)
        vertical += jnp.dot(diag_low, q_high, preferred_element_type=jnp.float32)
        vertical += jnp.dot(diag_high, q_low, preferred_element_type=jnp.float32)
        for i in range(nx):
            q = flow[f, i]
            slopes = jnp.zeros((nz, ny), jnp.float32)
            for offset, factor in ((1, 45.0 / 60.0), (2, -9.0 / 60.0), (3, 1.0 / 60.0)):
                slopes += factor * (pltpu.roll(q, ny - offset, 1) - pltpu.roll(q, offset, 1))
            tend = vertical[i * nz:(i + 1) * nz] - flow[1, i] * slopes
            tend_ref[f, i] = tend
            new_ref[f, i] = cour[i] * (q + STEP * tend)

    for halo in halos:
        halo.wait_recv()
    fixes = []
    for v in range(npack):
        low, high = packed[v]
        before = jnp.where(wid == 0, 0.0, halo_in[1, v]) - high
        after = jnp.where(wid == nwid - 1, 0.0, halo_in[0, v]) - low
        fix_low = (
            (-1.0 / 60.0) * before
            + jnp.where(spot < 2, 9.0 / 60.0, 0.0) * pltpu.roll(before, LANE - 1, 1)
            + jnp.where(spot < 1, -45.0 / 60.0, 0.0) * pltpu.roll(before, LANE - 2, 1)
        )
        fix_high = (
            (1.0 / 60.0) * after
            + jnp.where(spot >= 1, -9.0 / 60.0, 0.0) * pltpu.roll(after, 1, 1)
            + jnp.where(spot >= 2, 45.0 / 60.0, 0.0) * pltpu.roll(after, 2, 1)
        )
        fixes.append((fix_low, fix_high))

    def scatter(tile, v, h, l):
        send1[pl.ds(h * SUB * SUB + v * nl + l, SUB, stride=SUB), :] = tile

    for h in range(nh):
        z = slice(h * SUB, (h + 1) * SUB)
        for l in range(nl):
            y = slice(l * LANE, (l + 1) * LANE)
            scatter(prod[nx - 1, z, y], 0, h, l)
            for f in range(fields):
                state = None
                for i in range(nx):
                    v, s = divmod((f * nx + i) * nh + h, slots)
                    more = new_ref[f, i, z, y]
                    if l == 0 or l == nl - 1:
                        fix = jnp.zeros((SUB, LANE), jnp.float32)
                        if l == 0:
                            turned = pltpu.roll(fixes[v][0], LANE - 4 * s, 1) if s else fixes[v][0]
                            fix = jnp.where(lane < 3, turned, fix)
                        if l == nl - 1:
                            turned = pltpu.roll(fixes[v][1], (2 * LANE - 3 - 4 * s) % LANE, 1)
                            fix = jnp.where(lane >= LANE - 3, turned, fix)
                        tend_ref[f, i, z, y] -= flow[1, i, z, y] * fix
                        more -= gain[i, z, y] * fix
                    state = more if state is None else keep[i, z, y] * state + more
                    new_ref[f, i, z, y] = state
                scatter(state, 1 + f, h, l)

    def remote(source, target, phase, slot, device):
        return pltpu.make_async_remote_copy(
            src_ref=source,
            dst_ref=target,
            send_sem=ex_send.at[phase],
            recv_sem=ex_recv.at[slot],
            device_id=(device, wid),
            device_id_type=MESH,
        )

    def rows_of(k):
        return pl.ds(k * chunk if isinstance(k, int) else pl.multiple_of(k * chunk, SUB), chunk)

    def part(ref, k):
        return ref.at[rows_of(k), :]

    def total(ref, parts, phase, slot):
        span = ref.at[pl.ds(0, parts * chunk), :]
        return remote(span, span, phase, slot, me)

    def load_map(ref, at):
        tile = ref[at:at + SUB, :]
        decay = jnp.broadcast_to(tile[0:1], (SUB, LANE))
        for l in range(1, nl):
            decay = jnp.where(row % nl == l, jnp.broadcast_to(tile[l:l + 1], (SUB, LANE)), decay)
        return decay, tile

    section = lax.div(me, half)
    sections = 2 * outer
    back = sections
    for j in sorted(range(outer), key=lambda j: -min(j, outer - j)):
        to = lax.rem(block + j, outer)
        for r in range(deep):
            k = (SHIFT + r) % inner

            def give():
                remote(part(send1, to + outer * r), part(recv1, me), 0, section, to * inner + k).start()

            if j:
                give()
            else:
                pl.when(mine != k)(give)

    @pl.when(owner)
    def _():
        recv1[rows_of(me), :] = send1[rows_of(rank), :]
        entries = list(starts)

        def send_back(q):
            for t in range(q * half, (q + 1) * half):
                @pl.when(me != t)
                def _():
                    remote(part(send3, t), part(recv3, rank), 1, back, t).start()

        for q in range(sections):
            @pl.when(section == q)
            def _():
                total(recv1, half - 1, 0, q).wait_recv()

            @pl.when(section != q)
            def _():
                total(recv1, half, 0, q).wait_recv()

            for t in range(q * half, (q + 1) * half):
                for p in range(per):
                    at = t * chunk + p * SUB
                    send3[at:at + SUB, :] = entries[p]
                    decay, state = load_map(recv1, at)
                    entries[p] = decay * entries[p] + state
            if q % 2 == 0:
                send_back(q)
                if q:
                    send_back(q - 1)
        send_back(sections - 1)
        recv3[rows_of(rank), :] = send3[rows_of(me), :]
        total(recv3, owners - 1, 1, back).wait_recv()

    @pl.when(jnp.logical_not(owner))
    def _():
        total(recv3, owners, 1, back).wait_recv()

    for f in range(fields):
        for h in range(nh):
            for l in range(nl):
                enter = recv3[pl.ds(h * SUB * SUB + (1 + f) * nl + l, SUB, stride=SUB), :]
                z, y = slice(h * SUB, (h + 1) * SUB), slice(l * LANE, (l + 1) * LANE)
                for i in range(nx):
                    new_ref[f, i, z, y] += prod[i, z, y] * enter

    for halo in halos:
        halo.wait_send()

    @pl.when(owner)
    def _():
        total(send1, owners - 1, 0, 0).wait_send()
        total(send3, count - 1, 1, 0).wait_send()

    @pl.when(jnp.logical_not(owner))
    def _():
        total(send1, owners, 0, 0).wait_send()


def store_kernel(new_in, tend_in, new_out, tend_out, sem):
    copies = [
        pltpu.make_async_copy(src, dst, sem.at[i])
        for i, (src, dst) in enumerate(((new_in, new_out), (tend_in, tend_out)))
    ]
    for copy in copies:
        copy.start()
    for copy in copies:
        copy.wait()


def shards(inner, deep, flow_state, courant, inflow, height_ops, metric_index):
    fields, nx, nz, ny = flow_state.shape
    count = lax.axis_size("len")
    nwid = lax.axis_size("wid")
    outer = count // inner
    owners = deep * outer
    chunk = nz // owners * SUB
    out = jax.ShapeDtypeStruct(flow_state.shape, jnp.float32)
    anywhere = pl.BlockSpec(memory_space=pl.ANY)
    nrow = fields * nx * (nz // SUB)
    npack = pl.cdiv(nrow, LANE // 4)
    f32 = jnp.float32
    dma = pltpu.SemaphoreType.DMA
    held = [
        pltpu.with_memory_space_constraint(value, pltpu.HBM)
        for value in (flow_state, courant, inflow, height_ops, metric_index)
    ]
    new_state, tendency = pl.pallas_call(
        functools.partial(sweep_kernel, inner, outer, deep, nwid, metric_index.shape[0]),
        out_shape=(out, out),
        in_specs=[pl.BlockSpec(memory_space=pltpu.HBM)] * 5,
        out_specs=(pl.BlockSpec(memory_space=pltpu.VMEM),) * 2,
        scratch_shapes=[
            pltpu.VMEM(flow_state.shape, f32),
            pltpu.VMEM(courant.shape, f32),
            pltpu.VMEM(inflow.shape, f32),
            pltpu.VMEM(height_ops.shape, f32),
            pltpu.SMEM(metric_index.shape, jnp.int32),
            pltpu.VMEM(courant.shape, f32),
            pltpu.VMEM(courant.shape, f32),
            pltpu.VMEM(courant.shape, f32),
            pltpu.VMEM((2, npack, SUB, LANE), f32),
            pltpu.VMEM((2, npack, SUB, LANE), f32),
            pltpu.VMEM((owners * chunk, LANE), f32),
            pltpu.VMEM((count * chunk, LANE), f32),
            pltpu.VMEM((count * chunk, LANE), f32),
            pltpu.VMEM((owners * chunk, LANE), f32),
            dma((5,)),
            dma((2,)),
            dma((2,)),
            dma((2,)),
            dma((2 * outer + 1,)),
        ],
        compiler_params=pltpu.CompilerParams(
            collective_id=0, has_side_effects=True, vmem_limit_bytes=16 << 20
        ),
        name="sweep",
    )(*held)
    return pl.pallas_call(
        store_kernel,
        out_shape=(out, out),
        in_specs=[anywhere] * 2,
        out_specs=(anywhere, anywhere),
        scratch_shapes=[dma((2,))],
        compiler_params=pltpu.CompilerParams(vmem_limit_bytes=4 << 20),
        name="finish",
    )(new_state, tendency)


def solution(mesh, inner=16, deep=4):
    placed = (
        P(None, "len", None, "wid"),
        P("len", None, "wid"),
        P(None, None, "wid"),
        P(),
        P("len"),
    )
    return jax.shard_map(
        functools.partial(shards, inner, deep),
        mesh=mesh,
        in_specs=placed,
        out_specs=(P(None, "len", None, "wid"), P(None, "len", None, "wid")),
        check_vma=False,
    )
```

```python
import functools

import jax
import jax.numpy as jnp
from jax import lax
from jax.experimental import pallas as pl
from jax.experimental.pallas import tpu as pltpu
from jax.sharding import PartitionSpec as P

STEP = 0.25
SHIFT = 0
LANE = 128
SUB = 8
MESH = pl.DeviceIdType.MESH


def split_bf16(value):
    high = value.astype(jnp.bfloat16)
    return high, (value - high.astype(jnp.float32)).astype(jnp.bfloat16)


def sweep_kernel(
    inner, outer, deep, nwid, groups,
    flow_hbm, cour_hbm, inflow_hbm, ops_hbm, metric_hbm,
    new_ref, tend_ref,
    flow, cour, infl, ops, metric, prod, keep, gain, halo_out, halo_in,
    edge_out, edge_in, pull_out, pull_in, edge_tiles,
    send1, recv1, send3, recv3,
    in_sem, halo_send, halo_recv, edge_send, edge_recv, pull_send, pull_recv, ex_send, ex_recv,
):
    fields, nx, nz, ny = flow.shape
    nh, nl = nz // SUB, ny // LANE
    count = inner * outer
    owners = deep * outer
    per = nz // owners
    chunk = per * SUB
    half = inner // 2
    me = lax.axis_index("len")
    wid = lax.axis_index("wid")
    mine = lax.rem(me, inner)
    block = lax.div(me, inner)
    right, left = lax.rem(wid + 1, nwid), lax.rem(wid + nwid - 1, nwid)

    loads = [
        pltpu.make_async_copy(src, dst, in_sem.at[i])
        for i, (src, dst) in enumerate(
            ((flow_hbm, flow), (cour_hbm, cour), (inflow_hbm, infl), (ops_hbm, ops), (metric_hbm, metric))
        )
    ]
    for load in loads:
        load.start()

    place = lax.rem(mine + (inner - SHIFT), inner)
    owner = place < deep
    rank = block + outer * place

    def seat(w):
        return (w % outer) * inner + (SHIFT + w // outer) % inner

    barrier = pltpu.get_barrier_semaphore()

    def greet(to, across):
        pl.semaphore_signal(barrier, inc=1, device_id=(to, across), device_id_type=MESH)

    greet(me, left)
    greet(me, right)
    seats = [seat(w) for w in range(owners)]
    for t in seats:
        @pl.when(me != t)
        def _():
            greet(t, wid)

    @pl.when(owner)
    def _():
        for t in range(count):
            if t not in seats:
                greet(t, wid)
            greet(t, left)
            greet(t, right)

    row = lax.broadcasted_iota(jnp.int32, (SUB, LANE), 0)
    lane = lax.broadcasted_iota(jnp.int32, (SUB, LANE), 1)
    slot, spot = lane // 4, lane % 4
    section = lax.div(me, half)
    sections = 2 * outer
    field_lanes = nx * 4
    states = fields * nl
    back_rows = per * states

    ahead = lax.broadcasted_iota(jnp.int32, (ny, ny), 0) - lax.broadcasted_iota(jnp.int32, (ny, ny), 1)
    reach = jnp.abs(ahead)
    band = jnp.where(reach == 1, 45.0, jnp.where(reach == 2, -9.0, jnp.where(reach == 3, 1.0, 0.0)))
    band = jnp.where(ahead < 0, -band, band).astype(jnp.bfloat16)

    loads[0].wait()
    for h in range(nh):
        z = slice(h * SUB, (h + 1) * SUB)
        low = jnp.zeros((SUB, LANE), jnp.float32)
        high = low
        for f in range(fields):
            for i in range(nx):
                s = f * nx + i
                here = slot == s
                first, last = flow[f, i, z, :LANE], flow[f, i, z, ny - LANE:]
                low = jnp.where(here, pltpu.roll(first, 4 * s, 1) if s else first, low)
                high = jnp.where(here, pltpu.roll(last, (4 * s + 3) % LANE, 1), high)
        low = jnp.where(spot < 3, low, 0.0)
        high = jnp.where(spot < 3, high, 0.0)
        first = (
            (1.0 / 60.0) * low
            + jnp.where(spot >= 1, -9.0 / 60.0, 0.0) * pltpu.roll(low, 1, 1)
            + jnp.where(spot >= 2, 45.0 / 60.0, 0.0) * pltpu.roll(low, 2, 1)
        )
        last = (
            (-1.0 / 60.0) * high
            + jnp.where(spot < 2, 9.0 / 60.0, 0.0) * pltpu.roll(high, LANE - 1, 1)
            + jnp.where(spot < 1, -45.0 / 60.0, 0.0) * pltpu.roll(high, LANE - 2, 1)
        )
        first = jnp.where(spot < 3, first, 0.0)
        last = jnp.where(spot < 3, last, 0.0)
        halo_out[0, h] = first
        halo_out[1, h] = last
        edge_out[h * SUB:(h + 1) * SUB, 0, :] = first
        edge_out[nz + h * SUB:nz + (h + 1) * SUB, 0, :] = last

    @pl.when(owner)
    def _():
        pl.semaphore_wait(barrier, 2 + count - 1 + 2 * owners)

    @pl.when(jnp.logical_not(owner))
    def _():
        pl.semaphore_wait(barrier, 2 + 3 * owners)

    halos = [
        pltpu.make_async_remote_copy(
            src_ref=halo_out.at[side],
            dst_ref=halo_in.at[side],
            send_sem=halo_send.at[side],
            recv_sem=halo_recv.at[side],
            device_id=(me, to),
            device_id_type=MESH,
        )
        for side, to in ((0, left), (1, right))
    ]
    def far_first(act):
        for j in sorted(range(outer), key=lambda j: -min(j, outer - j)):
            to = lax.rem(block + j, outer)
            for r in range(deep):
                act(j, to + outer * r, to * inner + (SHIFT + r) % inner)

    def edge_copy(side, across, w, device, p):
        return pltpu.make_async_remote_copy(
            src_ref=edge_out.at[pl.ds(side * nz + w * per + p, 1)],
            dst_ref=edge_in.at[pl.ds(((1 - side) * per + p) * count + me, 1)],
            send_sem=edge_send,
            recv_sem=edge_recv.at[section],
            device_id=(device, across),
            device_id_type=MESH,
        )

    def give_edges(j, w, device):
        for p in range(per):
            edge_copy(0, left, w, device, p).start()
            edge_copy(1, right, w, device, p).start()

    far_first(give_edges)
    for halo in halos:
        halo.start()

    loads[4].wait()
    loads[3].wait()
    rows = nx * nz
    tiles = []
    for g in range(groups):
        one = ops[metric[g]]
        tiles.append(jnp.concatenate([one] * nx, axis=1))
    row_cell = lax.broadcasted_iota(jnp.int32, (nz, rows), 1) // nz
    diag = jnp.concatenate(
        [jnp.where(row_cell == i, tiles[i * groups // nx], 0.0) for i in range(nx)], axis=0
    )
    diag_high, diag_low = split_bf16(diag)

    loads[1].wait()
    for i in range(nx):
        c = cour[i]
        t = 1.0 / (1.0 + c)
        cour[i] = t
        k = jnp.where(c < 1.0, c * t, 1.0 - t)
        keep[i] = k
        gain[i] = STEP * t * flow[1, i]
        prod[i] = k if i == 0 else k * prod[i - 1]

    pulls = []
    after = None
    tiles = [jnp.zeros((SUB, LANE), jnp.float32) for _ in range(nh)]
    for i in reversed(range(nx)):
        weight = -gain[i] if after is None else -gain[i] * after
        after = keep[i] if after is None else after * keep[i]
        for h in range(nh):
            z = slice(h * SUB, (h + 1) * SUB)
            turned = pltpu.roll(weight[z, :LANE], 4 * i, 1) if i else weight[z, :LANE]
            tiles[h] = jnp.where(slot == i, turned, tiles[h])
            turned = pltpu.roll(weight[z, ny - LANE:], (4 * (nx + i) + 3) % LANE, 1)
            tiles[h] = jnp.where(slot == nx + i, turned, tiles[h])
    for h in range(nh):
        pulls.append(jnp.where(spot < 3, tiles[h], 0.0))
        pull_out[h * SUB:(h + 1) * SUB, 0, :] = pulls[h]

    def pull_copy(w, device, p):
        return pltpu.make_async_remote_copy(
            src_ref=pull_out.at[pl.ds(w * per + p, 1)],
            dst_ref=pull_in.at[pl.ds(p * count + me, 1)],
            send_sem=pull_send,
            recv_sem=pull_recv.at[section],
            device_id=(device, wid),
            device_id_type=MESH,
        )

    def give_pulls(j, w, device):
        def give():
            for p in range(per):
                pull_copy(w, device, p).start()

        if j:
            give()
        else:
            pl.when(me != device)(give)

    far_first(give_pulls)

    def edge_terms(at_start, at_end, pull):
        lanes = lax.broadcasted_iota(jnp.int32, pull.shape, 1)

        def summed(edges, weights):
            spread = weights
            for f in range(1, fields):
                spread = spread + pltpu.roll(weights, f * field_lanes, 1)
            value = edges * spread
            step = field_lanes // 2
            while step >= 4:
                value = value + pltpu.roll(value, LANE - step, 1)
                step //= 2
            return value

        begin = summed(at_start, jnp.where(lanes < field_lanes, pull, 0.0))
        moved = pltpu.roll(pull, LANE - field_lanes, 1)
        end = summed(at_end, jnp.where(lanes < field_lanes, moved, 0.0))
        terms = []
        for f in range(fields):
            turned = pltpu.roll(begin, LANE - f * field_lanes, 1) if f else begin
            first = jnp.where(lanes < 3, turned, 0.0)
            turned = pltpu.roll(end, (2 * LANE - 3 - f * field_lanes) % LANE, 1)
            terms.append((first, jnp.where(lanes >= LANE - 3, turned, 0.0)))
        return terms

    loads[2].wait()
    height = lax.broadcasted_iota(jnp.int32, (nz, LANE), 0)
    starts = []
    for p in range(per):
        tile = jnp.zeros((SUB, LANE), jnp.float32)
        for f in range(fields):
            for l in range(nl):
                line = jnp.where(height == rank * per + p, infl[f, :, l * LANE:(l + 1) * LANE], 0.0)
                line = jnp.sum(line, axis=0, keepdims=True)
                tile = jnp.where(row == f * nl + l, jnp.broadcast_to(line, (SUB, LANE)), tile)
        starts.append(tile)

    for f in range(fields):
        q_high, q_low = split_bf16(flow[f].reshape(rows, ny))
        vertical = jnp.dot(diag_high, q_high, preferred_element_type=jnp.float32)
        vertical += jnp.dot(diag_low, q_high, preferred_element_type=jnp.float32)
        vertical += jnp.dot(diag_high, q_low, preferred_element_type=jnp.float32)
        slopes = jnp.dot(q_high, band, preferred_element_type=jnp.float32)
        slopes += jnp.dot(q_low, band, preferred_element_type=jnp.float32)
        for i in range(nx):
            at = slice(i * nz, (i + 1) * nz)
            tend = vertical[at] - flow[1, i] * ((1.0 / 60.0) * slopes[at])
            tend_ref[f, i] = tend
            new_ref[f, i] = cour[i] * (flow[f, i] + STEP * tend)

    def scatter(tile, v, h, l):
        send1[pl.ds(h * SUB * SUB + v * nl + l, SUB, stride=SUB), :] = tile

    for h in range(nh):
        z = slice(h * SUB, (h + 1) * SUB)
        for l in range(nl):
            y = slice(l * LANE, (l + 1) * LANE)
            scatter(prod[nx - 1, z, y], fields, h, l)
            for f in range(fields):
                state = None
                for i in range(nx):
                    more = new_ref[f, i, z, y]
                    state = more if state is None else keep[i, z, y] * state + more
                    new_ref[f, i, z, y] = state
                scatter(state, f, h, l)

    def remote(source, target, phase, slot, device):
        return pltpu.make_async_remote_copy(
            src_ref=source,
            dst_ref=target,
            send_sem=ex_send.at[phase],
            recv_sem=ex_recv.at[slot],
            device_id=(device, wid),
            device_id_type=MESH,
        )

    def rows_of(k):
        return pl.ds(k * chunk if isinstance(k, int) else pl.multiple_of(k * chunk, SUB), chunk)

    def part(ref, k):
        return ref.at[rows_of(k), :]

    def total(ref, parts, phase, slot):
        span = ref.at[pl.ds(0, parts * chunk), :]
        return remote(span, span, phase, slot, me)

    def load_map(ref, at):
        tile = ref[at:at + SUB, :]
        decay = jnp.broadcast_to(tile[states:states + 1], (SUB, LANE))
        for l in range(1, nl):
            decay = jnp.where(row % nl == l, jnp.broadcast_to(tile[states + l:states + l + 1], (SUB, LANE)), decay)
        return decay, tile

    back = sections

    def back_part(ref, k):
        return ref.at[pl.ds(k * back_rows, back_rows)]

    def back_total(ref, parts):
        span = ref.at[pl.ds(0, parts * back_rows)]
        return remote(span, span, 1, back, me)

    def give_map(j, w, device):
        def give():
            remote(part(send1, w), part(recv1, me), 0, section, device).start()

        if j:
            give()
        else:
            pl.when(me != device)(give)

    far_first(give_map)

    for halo in halos:
        halo.wait_recv()
    for h in range(nh):
        z = slice(h * SUB, (h + 1) * SUB)
        fix_start = jnp.where(wid == 0, 0.0, halo_in[1, h])
        fix_end = jnp.where(wid == nwid - 1, 0.0, halo_in[0, h])
        for l in {0, nl - 1}:
            y = slice(l * LANE, (l + 1) * LANE)
            for f in range(fields):
                state = None
                for i in range(nx):
                    s = f * nx + i
                    fix = jnp.zeros((SUB, LANE), jnp.float32)
                    if l == 0:
                        turned = pltpu.roll(fix_start, LANE - 4 * s, 1) if s else fix_start
                        fix = jnp.where(lane < 3, turned, fix)
                    if l == nl - 1:
                        turned = pltpu.roll(fix_end, (2 * LANE - 3 - 4 * s) % LANE, 1)
                        fix = jnp.where(lane >= LANE - 3, turned, fix)
                    tend_ref[f, i, z, y] -= flow[1, i, z, y] * fix
                    more = gain[i, z, y] * fix
                    state = more if state is None else keep[i, z, y] * state + more
                    new_ref[f, i, z, y] -= state

    @pl.when(owner)
    def _():
        recv1[rows_of(me), :] = send1[rows_of(rank), :]
        for p in range(per):
            pull_in[pl.ds(p * count + me, 1)] = pull_out[pl.ds(rank * per + p, 1)]

        def pull_wait(parts, q):
            span = pull_in.at[pl.ds(0, parts * per)]
            pltpu.make_async_remote_copy(
                src_ref=span, dst_ref=span, send_sem=pull_send, recv_sem=pull_recv.at[q],
                device_id=(me, right), device_id_type=MESH,
            ).wait_recv()

        entries = list(starts)

        def send_back(q):
            for t in range(q * half, (q + 1) * half):
                def give():
                    remote(back_part(send3, t), back_part(recv3, rank), 1, back, t).start()

                if t in seats:
                    pl.when(me != t)(give)
                else:
                    give()

        for q in range(sections):
            @pl.when(section == q)
            def _():
                pull_wait(half - 1, q)
                total(recv1, half - 1, 0, q).wait_recv()

            @pl.when(section != q)
            def _():
                pull_wait(half, q)
                total(recv1, half, 0, q).wait_recv()

            span = edge_in.at[pl.ds(0, 2 * half * per)]
            pltpu.make_async_remote_copy(
                src_ref=span, dst_ref=span, send_sem=edge_send, recv_sem=edge_recv.at[q],
                device_id=(me, right), device_id_type=MESH,
            ).wait_recv()
            for p in range(per):
                at = p * count + q * half
                terms = edge_terms(
                    jnp.where(wid == 0, 0.0, edge_in[at:at + half, 0, :]),
                    jnp.where(wid == nwid - 1, 0.0, edge_in[per * count + at:per * count + at + half, 0, :]),
                    pull_in[at:at + half, 0, :],
                )
                for f in range(fields):
                    for l in range(nl):
                        term = jnp.zeros((half, LANE), jnp.float32)
                        if l == 0:
                            term += terms[f][0]
                        if l == nl - 1:
                            term += terms[f][1]
                        edge_tiles[pl.ds(at * SUB + f * nl + l, half, stride=SUB), :] = term

            for t in range(q * half, (q + 1) * half):
                for p in range(per):
                    at = t * chunk + p * SUB
                    send3[t * back_rows + p * states:t * back_rows + (p + 1) * states, 0, :] = entries[p][:states]
                    decay, state = load_map(recv1, at)
                    edge = edge_tiles[(p * count + t) * SUB:(p * count + t + 1) * SUB, :]
                    edge = jnp.where(row < states, edge, 0.0)
                    entries[p] = decay * entries[p] + (state + edge)
            if q % 2 == 0:
                send_back(q)
                if q > 2:
                    send_back(q - 3)
        send_back(sections - 3)
        send_back(sections - 1)
        recv3[pl.ds(rank * back_rows, back_rows)] = send3[pl.ds(me * back_rows, back_rows)]
        back_total(recv3, owners - 1).wait_recv()

    @pl.when(jnp.logical_not(owner))
    def _():
        back_total(recv3, owners).wait_recv()

    for f in range(fields):
        for h in range(nh):
            for l in range(nl):
                enter = recv3[pl.ds(h * SUB * states + f * nl + l, SUB, stride=states), 0, :]
                z, y = slice(h * SUB, (h + 1) * SUB), slice(l * LANE, (l + 1) * LANE)
                for i in range(nx):
                    new_ref[f, i, z, y] += prod[i, z, y] * enter

    for halo in halos:
        halo.wait_send()
    span = edge_in.at[pl.ds(0, 2 * owners * per)]
    pltpu.make_async_remote_copy(
        src_ref=span, dst_ref=span, send_sem=edge_send, recv_sem=edge_recv.at[0],
        device_id=(me, right), device_id_type=MESH,
    ).wait_send()

    def pull_sent(parts):
        span = pull_in.at[pl.ds(0, parts * per)]
        pltpu.make_async_remote_copy(
            src_ref=span, dst_ref=span, send_sem=pull_send, recv_sem=pull_recv.at[0],
            device_id=(me, right), device_id_type=MESH,
        ).wait_send()

    @pl.when(owner)
    def _():
        pull_sent(owners - 1)
        total(send1, owners - 1, 0, 0).wait_send()
        back_total(send3, count - 1).wait_send()

    @pl.when(jnp.logical_not(owner))
    def _():
        pull_sent(owners)
        total(send1, owners, 0, 0).wait_send()


def store_kernel(new_in, tend_in, new_out, tend_out, sem):
    copies = [
        pltpu.make_async_copy(src, dst, sem.at[i])
        for i, (src, dst) in enumerate(((new_in, new_out), (tend_in, tend_out)))
    ]
    for copy in copies:
        copy.start()
    for copy in copies:
        copy.wait()


def shards(inner, deep, flow_state, courant, inflow, height_ops, metric_index):
    fields, nx, nz, ny = flow_state.shape
    count = lax.axis_size("len")
    nwid = lax.axis_size("wid")
    outer = count // inner
    owners = deep * outer
    chunk = nz // owners * SUB
    out = jax.ShapeDtypeStruct(flow_state.shape, jnp.float32)
    anywhere = pl.BlockSpec(memory_space=pl.ANY)
    nh = nz // SUB
    states = fields * (ny // LANE)
    heights = nz // owners * count
    f32 = jnp.float32
    dma = pltpu.SemaphoreType.DMA
    held = [
        pltpu.with_memory_space_constraint(value, pltpu.HBM)
        for value in (flow_state, courant, inflow, height_ops, metric_index)
    ]
    new_state, tendency = pl.pallas_call(
        functools.partial(sweep_kernel, inner, outer, deep, nwid, metric_index.shape[0]),
        out_shape=(out, out),
        in_specs=[pl.BlockSpec(memory_space=pltpu.HBM)] * 5,
        out_specs=(pl.BlockSpec(memory_space=pltpu.VMEM),) * 2,
        scratch_shapes=[
            pltpu.VMEM(flow_state.shape, f32),
            pltpu.VMEM(courant.shape, f32),
            pltpu.VMEM(inflow.shape, f32),
            pltpu.VMEM(height_ops.shape, f32),
            pltpu.SMEM(metric_index.shape, jnp.int32),
            pltpu.VMEM(courant.shape, f32),
            pltpu.VMEM(courant.shape, f32),
            pltpu.VMEM(courant.shape, f32),
            pltpu.VMEM((2, nh, SUB, LANE), f32),
            pltpu.VMEM((2, nh, SUB, LANE), f32),
            pltpu.VMEM((2 * nz, 1, LANE), f32),
            pltpu.VMEM((2 * heights, 1, LANE), f32),
            pltpu.VMEM((nz, 1, LANE), f32),
            pltpu.VMEM((heights, 1, LANE), f32),
            pltpu.VMEM((heights * SUB, LANE), f32),
            pltpu.VMEM((owners * chunk, LANE), f32),
            pltpu.VMEM((count * chunk, LANE), f32),
            pltpu.VMEM((heights * states, 1, LANE), f32),
            pltpu.VMEM((nz * states, 1, LANE), f32),
            dma((5,)),
            dma((2,)),
            dma((2,)),
            dma,
            dma((2 * outer,)),
            dma,
            dma((2 * outer,)),
            dma((2,)),
            dma((2 * outer + 1,)),
        ],
        compiler_params=pltpu.CompilerParams(
            collective_id=0, has_side_effects=True, vmem_limit_bytes=16 << 20
        ),
        name="sweep",
    )(*held)
    return pl.pallas_call(
        store_kernel,
        out_shape=(out, out),
        in_specs=[anywhere] * 2,
        out_specs=(anywhere, anywhere),
        scratch_shapes=[dma((2,))],
        compiler_params=pltpu.CompilerParams(vmem_limit_bytes=4 << 20),
        name="finish",
    )(new_state, tendency)


def solution(mesh, inner=16, deep=4):
    placed = (
        P(None, "len", None, "wid"),
        P("len", None, "wid"),
        P(None, None, "wid"),
        P(),
        P("len"),
    )
    return jax.shard_map(
        functools.partial(shards, inner, deep),
        mesh=mesh,
        in_specs=placed,
        out_specs=(P(None, "len", None, "wid"), P(None, "len", None, "wid")),
        check_vma=False,
    )
```

```python
import functools

import jax
import jax.numpy as jnp
from jax import lax
from jax.experimental import pallas as pl
from jax.experimental.pallas import tpu as pltpu
from jax.sharding import PartitionSpec as P

STEP = 0.25
SHIFT = 0
LANE = 128
SUB = 8
MESH = pl.DeviceIdType.MESH


def split_bf16(value):
    high = value.astype(jnp.bfloat16)
    return high, (value - high.astype(jnp.float32)).astype(jnp.bfloat16)


def sweep_kernel(
    inner, outer, deep, nwid, groups,
    flow_hbm, cour_hbm, inflow_hbm, ops_hbm, metric_hbm,
    new_ref, tend_ref,
    flow, cour, infl, ops, metric, prod, keep, gain, halo_out, halo_in,
    edge_out, edge_in, pull_out, pull_in, edge_tiles,
    send1, recv1, send3, recv3,
    in_sem, halo_send, halo_recv, edge_send, edge_recv, pull_send, pull_recv, ex_send, ex_recv,
):
    fields, nx, nz, ny = flow.shape
    nh, nl = nz // SUB, ny // LANE
    count = inner * outer
    owners = deep * outer
    per = nz // owners
    chunk = per * SUB
    half = inner // 2
    me = lax.axis_index("len")
    wid = lax.axis_index("wid")
    mine = lax.rem(me, inner)
    block = lax.div(me, inner)
    right, left = jnp.minimum(wid + 1, nwid - 1), jnp.maximum(wid - 1, 0)
    has_left, has_right = wid > 0, wid < nwid - 1
    beside = jnp.where(has_left, 1, 0) + jnp.where(has_right, 1, 0)

    loads = [
        pltpu.make_async_copy(src, dst, in_sem.at[i])
        for i, (src, dst) in enumerate(
            ((flow_hbm, flow), (cour_hbm, cour), (inflow_hbm, infl), (ops_hbm, ops), (metric_hbm, metric))
        )
    ]
    for load in loads:
        load.start()

    place = lax.rem(mine + (inner - SHIFT), inner)
    owner = place < deep
    rank = block + outer * place

    def seat(w):
        return (w % outer) * inner + (SHIFT + w // outer) % inner

    barrier = pltpu.get_barrier_semaphore()

    def greet(to, across):
        pl.semaphore_signal(barrier, inc=1, device_id=(to, across), device_id_type=MESH)

    @pl.when(has_left)
    def _():
        greet(me, left)

    @pl.when(has_right)
    def _():
        greet(me, right)

    seats = [seat(w) for w in range(owners)]
    for t in seats:
        @pl.when(me != t)
        def _():
            greet(t, wid)

    @pl.when(owner)
    def _():
        for t in range(count):
            if t not in seats:
                greet(t, wid)

    @pl.when(jnp.logical_and(owner, has_left))
    def _():
        for t in range(count):
            greet(t, left)

    @pl.when(jnp.logical_and(owner, has_right))
    def _():
        for t in range(count):
            greet(t, right)

    @pl.when(jnp.logical_not(has_left))
    def _():
        halo_in[1] = jnp.zeros_like(halo_in[1])
        edge_in[:per * count] = jnp.zeros((per * count, 1, LANE), jnp.float32)

    @pl.when(jnp.logical_not(has_right))
    def _():
        halo_in[0] = jnp.zeros_like(halo_in[0])
        edge_in[per * count:] = jnp.zeros((per * count, 1, LANE), jnp.float32)

    row = lax.broadcasted_iota(jnp.int32, (SUB, LANE), 0)
    lane = lax.broadcasted_iota(jnp.int32, (SUB, LANE), 1)
    slot, spot = lane // 4, lane % 4
    section = lax.div(me, half)
    sections = 2 * outer
    field_lanes = nx * 4
    states = fields * nl
    back_rows = per * states

    ahead = lax.broadcasted_iota(jnp.int32, (ny, ny), 0) - lax.broadcasted_iota(jnp.int32, (ny, ny), 1)
    reach = jnp.abs(ahead)
    band = jnp.where(reach == 1, 45.0, jnp.where(reach == 2, -9.0, jnp.where(reach == 3, 1.0, 0.0)))
    band = jnp.where(ahead < 0, -band, band).astype(jnp.bfloat16)

    loads[0].wait()
    for h in range(nh):
        z = slice(h * SUB, (h + 1) * SUB)
        low = jnp.zeros((SUB, LANE), jnp.float32)
        high = low
        for f in range(fields):
            for i in range(nx):
                s = f * nx + i
                here = slot == s
                first, last = flow[f, i, z, :LANE], flow[f, i, z, ny - LANE:]
                low = jnp.where(here, pltpu.roll(first, 4 * s, 1) if s else first, low)
                high = jnp.where(here, pltpu.roll(last, (4 * s + 3) % LANE, 1), high)
        low = jnp.where(spot < 3, low, 0.0)
        high = jnp.where(spot < 3, high, 0.0)
        first = (
            (1.0 / 60.0) * low
            + jnp.where(spot >= 1, -9.0 / 60.0, 0.0) * pltpu.roll(low, 1, 1)
            + jnp.where(spot >= 2, 45.0 / 60.0, 0.0) * pltpu.roll(low, 2, 1)
        )
        last = (
            (-1.0 / 60.0) * high
            + jnp.where(spot < 2, 9.0 / 60.0, 0.0) * pltpu.roll(high, LANE - 1, 1)
            + jnp.where(spot < 1, -45.0 / 60.0, 0.0) * pltpu.roll(high, LANE - 2, 1)
        )
        first = jnp.where(spot < 3, first, 0.0)
        last = jnp.where(spot < 3, last, 0.0)
        halo_out[0, h] = first
        halo_out[1, h] = last
        edge_out[h * SUB:(h + 1) * SUB, 0, :] = first
        edge_out[nz + h * SUB:nz + (h + 1) * SUB, 0, :] = last

    @pl.when(owner)
    def _():
        pl.semaphore_wait(barrier, count - 1 + (1 + owners) * beside)

    @pl.when(jnp.logical_not(owner))
    def _():
        pl.semaphore_wait(barrier, owners + (1 + owners) * beside)

    halos = [
        pltpu.make_async_remote_copy(
            src_ref=halo_out.at[side],
            dst_ref=halo_in.at[side],
            send_sem=halo_send.at[side],
            recv_sem=halo_recv.at[side],
            device_id=(me, to),
            device_id_type=MESH,
        )
        for side, to in ((0, left), (1, right))
    ]
    def to_owners(act):
        for j in range(outer):
            to = lax.rem(block + j, outer)
            for r in reversed(range(deep)):
                act(j, to + outer * r, to * inner + (SHIFT + r) % inner)

    def edge_copy(side, across, w, device, p):
        return pltpu.make_async_remote_copy(
            src_ref=edge_out.at[pl.ds(side * nz + w * per + p, 1)],
            dst_ref=edge_in.at[pl.ds(((1 - side) * per + p) * count + me, 1)],
            send_sem=edge_send,
            recv_sem=edge_recv.at[section],
            device_id=(device, across),
            device_id_type=MESH,
        )

    def edge_span(parts, q):
        span = edge_in.at[pl.ds(0, parts * per)]
        return pltpu.make_async_remote_copy(
            src_ref=span, dst_ref=span, send_sem=edge_send, recv_sem=edge_recv.at[q],
            device_id=(me, wid), device_id_type=MESH,
        )

    def give_edges(j, w, device):
        for p in range(per):
            @pl.when(has_left)
            def _():
                edge_copy(0, left, w, device, p).start()

            @pl.when(has_right)
            def _():
                edge_copy(1, right, w, device, p).start()

    to_owners(give_edges)
    def each_halo(sent, got):
        for there, go, come in ((has_left, 0, 1), (has_right, 1, 0)):
            @pl.when(there)
            def _():
                if sent:
                    sent(halos[go])
                if got:
                    got(halos[come])

    each_halo(lambda halo: halo.start(), None)

    loads[4].wait()
    loads[3].wait()
    rows = nx * nz
    tiles = []
    for g in range(groups):
        one = ops[metric[g]]
        tiles.append(jnp.concatenate([one] * nx, axis=1))
    row_cell = lax.broadcasted_iota(jnp.int32, (nz, rows), 1) // nz
    diag = jnp.concatenate(
        [jnp.where(row_cell == i, tiles[i * groups // nx], 0.0) for i in range(nx)], axis=0
    )
    diag_high, diag_low = split_bf16(diag)

    loads[1].wait()
    for i in range(nx):
        c = cour[i]
        t = 1.0 / (1.0 + c)
        cour[i] = t
        k = jnp.where(c < 1.0, c * t, 1.0 - t)
        keep[i] = k
        gain[i] = STEP * t * flow[1, i]
        prod[i] = k if i == 0 else k * prod[i - 1]

    pulls = []
    after = None
    tiles = [jnp.zeros((SUB, LANE), jnp.float32) for _ in range(nh)]
    for i in reversed(range(nx)):
        weight = -gain[i] if after is None else -gain[i] * after
        after = keep[i] if after is None else after * keep[i]
        for h in range(nh):
            z = slice(h * SUB, (h + 1) * SUB)
            turned = pltpu.roll(weight[z, :LANE], 4 * i, 1) if i else weight[z, :LANE]
            tiles[h] = jnp.where(slot == i, turned, tiles[h])
            turned = pltpu.roll(weight[z, ny - LANE:], (4 * (nx + i) + 3) % LANE, 1)
            tiles[h] = jnp.where(slot == nx + i, turned, tiles[h])
    for h in range(nh):
        pulls.append(jnp.where(spot < 3, tiles[h], 0.0))
        pull_out[h * SUB:(h + 1) * SUB, 0, :] = pulls[h]

    def pull_copy(w, device, p):
        return pltpu.make_async_remote_copy(
            src_ref=pull_out.at[pl.ds(w * per + p, 1)],
            dst_ref=pull_in.at[pl.ds(p * count + me, 1)],
            send_sem=pull_send,
            recv_sem=pull_recv.at[section],
            device_id=(device, wid),
            device_id_type=MESH,
        )

    def give_pulls(j, w, device):
        def give():
            for p in range(per):
                pull_copy(w, device, p).start()

        if j:
            give()
        else:
            pl.when(me != device)(give)

    to_owners(give_pulls)

    def edge_terms(at_start, at_end, pull):
        lanes = lax.broadcasted_iota(jnp.int32, pull.shape, 1)

        def summed(edges, weights):
            spread = weights
            for f in range(1, fields):
                spread = spread + pltpu.roll(weights, f * field_lanes, 1)
            value = edges * spread
            step = field_lanes // 2
            while step >= 4:
                value = value + pltpu.roll(value, LANE - step, 1)
                step //= 2
            return value

        begin = summed(at_start, jnp.where(lanes < field_lanes, pull, 0.0))
        moved = pltpu.roll(pull, LANE - field_lanes, 1)
        end = summed(at_end, jnp.where(lanes < field_lanes, moved, 0.0))
        terms = []
        for f in range(fields):
            turned = pltpu.roll(begin, LANE - f * field_lanes, 1) if f else begin
            first = jnp.where(lanes < 3, turned, 0.0)
            turned = pltpu.roll(end, (2 * LANE - 3 - f * field_lanes) % LANE, 1)
            terms.append((first, jnp.where(lanes >= LANE - 3, turned, 0.0)))
        return terms

    loads[2].wait()
    height = lax.broadcasted_iota(jnp.int32, (nz, LANE), 0)
    starts = []
    for p in range(per):
        tile = jnp.zeros((SUB, LANE), jnp.float32)
        for f in range(fields):
            for l in range(nl):
                line = jnp.where(height == rank * per + p, infl[f, :, l * LANE:(l + 1) * LANE], 0.0)
                line = jnp.sum(line, axis=0, keepdims=True)
                tile = jnp.where(row == f * nl + l, jnp.broadcast_to(line, (SUB, LANE)), tile)
        starts.append(tile)

    for f in range(fields):
        q_high, q_low = split_bf16(flow[f].reshape(rows, ny))
        vertical = jnp.dot(diag_high, q_high, preferred_element_type=jnp.float32)
        vertical += jnp.dot(diag_low, q_high, preferred_element_type=jnp.float32)
        vertical += jnp.dot(diag_high, q_low, preferred_element_type=jnp.float32)
        slopes = jnp.dot(q_high, band, preferred_element_type=jnp.float32)
        slopes += jnp.dot(q_low, band, preferred_element_type=jnp.float32)
        for i in range(nx):
            at = slice(i * nz, (i + 1) * nz)
            tend = vertical[at] - flow[1, i] * ((1.0 / 60.0) * slopes[at])
            tend_ref[f, i] = tend
            new_ref[f, i] = cour[i] * (flow[f, i] + STEP * tend)

    def scatter(tile, v, h, l):
        send1[pl.ds(h * SUB * SUB + v * nl + l, SUB, stride=SUB), :] = tile

    for h in range(nh):
        z = slice(h * SUB, (h + 1) * SUB)
        for l in range(nl):
            y = slice(l * LANE, (l + 1) * LANE)
            scatter(prod[nx - 1, z, y], fields, h, l)
            for f in range(fields):
                state = None
                for i in range(nx):
                    more = new_ref[f, i, z, y]
                    state = more if state is None else keep[i, z, y] * state + more
                    new_ref[f, i, z, y] = state
                scatter(state, f, h, l)

    def remote(source, target, phase, slot, device):
        return pltpu.make_async_remote_copy(
            src_ref=source,
            dst_ref=target,
            send_sem=ex_send.at[phase],
            recv_sem=ex_recv.at[slot],
            device_id=(device, wid),
            device_id_type=MESH,
        )

    def rows_of(k):
        return pl.ds(k * chunk if isinstance(k, int) else pl.multiple_of(k * chunk, SUB), chunk)

    def part(ref, k):
        return ref.at[rows_of(k), :]

    def total(ref, parts, phase, slot):
        span = ref.at[pl.ds(0, parts * chunk), :]
        return remote(span, span, phase, slot, me)

    def load_map(ref, at):
        tile = ref[at:at + SUB, :]
        decay = jnp.broadcast_to(tile[states:states + 1], (SUB, LANE))
        for l in range(1, nl):
            decay = jnp.where(row % nl == l, jnp.broadcast_to(tile[states + l:states + l + 1], (SUB, LANE)), decay)
        return decay, tile

    back = sections

    def back_part(ref, k):
        return ref.at[pl.ds(k * back_rows, back_rows)]

    def back_total(ref, parts):
        span = ref.at[pl.ds(0, parts * back_rows)]
        return remote(span, span, 1, back, me)

    def give_map(j, w, device):
        def give():
            remote(part(send1, w), part(recv1, me), 0, section, device).start()

        if j:
            give()
        else:
            pl.when(me != device)(give)

    to_owners(give_map)

    each_halo(None, lambda halo: halo.wait_recv())
    for h in range(nh):
        z = slice(h * SUB, (h + 1) * SUB)
        fix_start = halo_in[1, h]
        fix_end = halo_in[0, h]
        for l in {0, nl - 1}:
            y = slice(l * LANE, (l + 1) * LANE)
            for f in range(fields):
                state = None
                for i in range(nx):
                    s = f * nx + i
                    fix = jnp.zeros((SUB, LANE), jnp.float32)
                    if l == 0:
                        turned = pltpu.roll(fix_start, LANE - 4 * s, 1) if s else fix_start
                        fix = jnp.where(lane < 3, turned, fix)
                    if l == nl - 1:
                        turned = pltpu.roll(fix_end, (2 * LANE - 3 - 4 * s) % LANE, 1)
                        fix = jnp.where(lane >= LANE - 3, turned, fix)
                    tend_ref[f, i, z, y] -= flow[1, i, z, y] * fix
                    more = gain[i, z, y] * fix
                    state = more if state is None else keep[i, z, y] * state + more
                    new_ref[f, i, z, y] -= state

    @pl.when(owner)
    def _():
        recv1[rows_of(me), :] = send1[rows_of(rank), :]
        for p in range(per):
            pull_in[pl.ds(p * count + me, 1)] = pull_out[pl.ds(rank * per + p, 1)]

        def pull_wait(parts, q):
            span = pull_in.at[pl.ds(0, parts * per)]
            pltpu.make_async_remote_copy(
                src_ref=span, dst_ref=span, send_sem=pull_send, recv_sem=pull_recv.at[q],
                device_id=(me, wid), device_id_type=MESH,
            ).wait_recv()

        entries = list(starts)

        def send_back(q):
            for t in range(q * half, (q + 1) * half):
                def give():
                    remote(back_part(send3, t), back_part(recv3, rank), 1, back, t).start()

                if t in seats:
                    pl.when(me != t)(give)
                else:
                    give()

        for q in range(sections):
            @pl.when(section == q)
            def _():
                pull_wait(half - 1, q)
                total(recv1, half - 1, 0, q).wait_recv()

            @pl.when(section != q)
            def _():
                pull_wait(half, q)
                total(recv1, half, 0, q).wait_recv()

            for sides in (1, 2):
                @pl.when(beside == sides)
                def _():
                    edge_span(sides * half, q).wait_recv()

            for p in range(per):
                at = p * count + q * half
                terms = edge_terms(
                    edge_in[at:at + half, 0, :],
                    edge_in[per * count + at:per * count + at + half, 0, :],
                    pull_in[at:at + half, 0, :],
                )
                for f in range(fields):
                    for l in range(nl):
                        term = jnp.zeros((half, LANE), jnp.float32)
                        if l == 0:
                            term += terms[f][0]
                        if l == nl - 1:
                            term += terms[f][1]
                        edge_tiles[pl.ds(at * SUB + f * nl + l, half, stride=SUB), :] = term

            for t in range(q * half, (q + 1) * half):
                for p in range(per):
                    at = t * chunk + p * SUB
                    send3[t * back_rows + p * states:t * back_rows + (p + 1) * states, 0, :] = entries[p][:states]
                    decay, state = load_map(recv1, at)
                    edge = edge_tiles[(p * count + t) * SUB:(p * count + t + 1) * SUB, :]
                    edge = jnp.where(row < states, edge, 0.0)
                    entries[p] = decay * entries[p] + (state + edge)
            if q % 2 == 0:
                send_back(q)
                if q > 2:
                    send_back(q - 3)
        send_back(sections - 3)
        send_back(sections - 1)
        recv3[pl.ds(rank * back_rows, back_rows)] = send3[pl.ds(me * back_rows, back_rows)]
        back_total(recv3, owners - 1).wait_recv()

    @pl.when(jnp.logical_not(owner))
    def _():
        back_total(recv3, owners).wait_recv()

    for f in range(fields):
        for h in range(nh):
            for l in range(nl):
                enter = recv3[pl.ds(h * SUB * states + f * nl + l, SUB, stride=states), 0, :]
                z, y = slice(h * SUB, (h + 1) * SUB), slice(l * LANE, (l + 1) * LANE)
                for i in range(nx):
                    new_ref[f, i, z, y] += prod[i, z, y] * enter

    each_halo(lambda halo: halo.wait_send(), None)
    for sides in (1, 2):
        @pl.when(beside == sides)
        def _():
            edge_span(sides * owners, 0).wait_send()

    def pull_sent(parts):
        span = pull_in.at[pl.ds(0, parts * per)]
        pltpu.make_async_remote_copy(
            src_ref=span, dst_ref=span, send_sem=pull_send, recv_sem=pull_recv.at[0],
            device_id=(me, wid), device_id_type=MESH,
        ).wait_send()

    @pl.when(owner)
    def _():
        pull_sent(owners - 1)
        total(send1, owners - 1, 0, 0).wait_send()
        back_total(send3, count - 1).wait_send()

    @pl.when(jnp.logical_not(owner))
    def _():
        pull_sent(owners)
        total(send1, owners, 0, 0).wait_send()


def store_kernel(new_in, tend_in, new_out, tend_out, sem):
    copies = [
        pltpu.make_async_copy(src, dst, sem.at[i])
        for i, (src, dst) in enumerate(((new_in, new_out), (tend_in, tend_out)))
    ]
    for copy in copies:
        copy.start()
    for copy in copies:
        copy.wait()


def shards(inner, deep, flow_state, courant, inflow, height_ops, metric_index):
    fields, nx, nz, ny = flow_state.shape
    count = lax.axis_size("len")
    nwid = lax.axis_size("wid")
    outer = count // inner
    owners = deep * outer
    chunk = nz // owners * SUB
    out = jax.ShapeDtypeStruct(flow_state.shape, jnp.float32)
    anywhere = pl.BlockSpec(memory_space=pl.ANY)
    nh = nz // SUB
    states = fields * (ny // LANE)
    heights = nz // owners * count
    f32 = jnp.float32
    dma = pltpu.SemaphoreType.DMA
    held = [
        pltpu.with_memory_space_constraint(value, pltpu.HBM)
        for value in (flow_state, courant, inflow, height_ops, metric_index)
    ]
    new_state, tendency = pl.pallas_call(
        functools.partial(sweep_kernel, inner, outer, deep, nwid, metric_index.shape[0]),
        out_shape=(out, out),
        in_specs=[pl.BlockSpec(memory_space=pltpu.HBM)] * 5,
        out_specs=(pl.BlockSpec(memory_space=pltpu.VMEM),) * 2,
        scratch_shapes=[
            pltpu.VMEM(flow_state.shape, f32),
            pltpu.VMEM(courant.shape, f32),
            pltpu.VMEM(inflow.shape, f32),
            pltpu.VMEM(height_ops.shape, f32),
            pltpu.SMEM(metric_index.shape, jnp.int32),
            pltpu.VMEM(courant.shape, f32),
            pltpu.VMEM(courant.shape, f32),
            pltpu.VMEM(courant.shape, f32),
            pltpu.VMEM((2, nh, SUB, LANE), f32),
            pltpu.VMEM((2, nh, SUB, LANE), f32),
            pltpu.VMEM((2 * nz, 1, LANE), f32),
            pltpu.VMEM((2 * heights, 1, LANE), f32),
            pltpu.VMEM((nz, 1, LANE), f32),
            pltpu.VMEM((heights, 1, LANE), f32),
            pltpu.VMEM((heights * SUB, LANE), f32),
            pltpu.VMEM((owners * chunk, LANE), f32),
            pltpu.VMEM((count * chunk, LANE), f32),
            pltpu.VMEM((heights * states, 1, LANE), f32),
            pltpu.VMEM((nz * states, 1, LANE), f32),
            dma((5,)),
            dma((2,)),
            dma((2,)),
            dma,
            dma((2 * outer,)),
            dma,
            dma((2 * outer,)),
            dma((2,)),
            dma((2 * outer + 1,)),
        ],
        compiler_params=pltpu.CompilerParams(
            collective_id=0, has_side_effects=True, vmem_limit_bytes=16 << 20
        ),
        name="sweep",
    )(*held)
    return pl.pallas_call(
        store_kernel,
        out_shape=(out, out),
        in_specs=[anywhere] * 2,
        out_specs=(anywhere, anywhere),
        scratch_shapes=[dma((2,))],
        compiler_params=pltpu.CompilerParams(vmem_limit_bytes=4 << 20),
        name="finish",
    )(new_state, tendency)


def solution(mesh, inner=16, deep=4):
    placed = (
        P(None, "len", None, "wid"),
        P("len", None, "wid"),
        P(None, None, "wid"),
        P(),
        P("len"),
    )
    return jax.shard_map(
        functools.partial(shards, inner, deep),
        mesh=mesh,
        in_specs=placed,
        out_specs=(P(None, "len", None, "wid"), P(None, "len", None, "wid")),
        check_vma=False,
    )
```

```python
import functools

import jax
import jax.numpy as jnp
from jax import lax
from jax.experimental import pallas as pl
from jax.experimental.pallas import tpu as pltpu
from jax.sharding import PartitionSpec as P

STEP = 0.25
SHIFT = 0
LANE = 128
SUB = 8
MESH = pl.DeviceIdType.MESH


def split_bf16(value):
    high = value.astype(jnp.bfloat16)
    return high, (value - high.astype(jnp.float32)).astype(jnp.bfloat16)


def sweep_kernel(
    inner, outer, deep, nwid, groups,
    flow_hbm, cour_hbm, inflow_hbm, ops_hbm, metric_hbm,
    new_ref, tend_ref,
    flow, cour, infl, ops, metric, prod, keep, gain, halo_out, halo_in,
    edge_out, edge_in, edge_tiles,
    send1, recv1, send3, recv3,
    in_sem, halo_send, halo_recv, edge_send, edge_recv, ex_send, ex_recv,
):
    fields, nx, nz, ny = flow.shape
    nh, nl = nz // SUB, ny // LANE
    count = inner * outer
    owners = deep * outer
    per = nz // owners
    half = inner // 2
    me = lax.axis_index("len")
    wid = lax.axis_index("wid")
    mine = lax.rem(me, inner)
    block = lax.div(me, inner)
    right, left = jnp.minimum(wid + 1, nwid - 1), jnp.maximum(wid - 1, 0)
    has_left, has_right = wid > 0, wid < nwid - 1
    beside = jnp.where(has_left, 1, 0) + jnp.where(has_right, 1, 0)

    loads = [
        pltpu.make_async_copy(src, dst, in_sem.at[i])
        for i, (src, dst) in enumerate(
            ((flow_hbm, flow), (cour_hbm, cour), (inflow_hbm, infl), (ops_hbm, ops), (metric_hbm, metric))
        )
    ]
    for load in loads:
        load.start()

    place = lax.rem(mine + (inner - SHIFT), inner)
    owner = place < deep
    rank = block + outer * place

    def seat(w):
        return (w % outer) * inner + (SHIFT + w // outer) % inner

    barrier = pltpu.get_barrier_semaphore()

    def greet(to, across):
        pl.semaphore_signal(barrier, inc=1, device_id=(to, across), device_id_type=MESH)

    @pl.when(has_left)
    def _():
        greet(me, left)

    @pl.when(has_right)
    def _():
        greet(me, right)

    seats = [seat(w) for w in range(owners)]
    for t in seats:
        @pl.when(me != t)
        def _():
            greet(t, wid)

    @pl.when(owner)
    def _():
        for t in range(count):
            if t not in seats:
                greet(t, wid)

    @pl.when(jnp.logical_and(owner, has_left))
    def _():
        for t in range(count):
            greet(t, left)

    @pl.when(jnp.logical_and(owner, has_right))
    def _():
        for t in range(count):
            greet(t, right)

    @pl.when(jnp.logical_not(has_left))
    def _():
        halo_in[1] = jnp.zeros_like(halo_in[1])
        edge_in[:per * count] = jnp.zeros((per * count, 1, LANE), jnp.float32)

    @pl.when(jnp.logical_not(has_right))
    def _():
        halo_in[0] = jnp.zeros_like(halo_in[0])
        edge_in[per * count:] = jnp.zeros((per * count, 1, LANE), jnp.float32)

    row = lax.broadcasted_iota(jnp.int32, (SUB, LANE), 0)
    lane = lax.broadcasted_iota(jnp.int32, (SUB, LANE), 1)
    slot, spot = lane // 4, lane % 4
    section = lax.div(me, half)
    sections = 2 * outer
    field_lanes = nx * 4
    states = fields * nl
    full = states + 1 + nl
    chunk = per * full
    back_rows = per * states

    ahead = lax.broadcasted_iota(jnp.int32, (ny, ny), 0) - lax.broadcasted_iota(jnp.int32, (ny, ny), 1)
    reach = jnp.abs(ahead)
    band = jnp.where(reach == 1, 45.0, jnp.where(reach == 2, -9.0, jnp.where(reach == 3, 1.0, 0.0)))
    band = jnp.where(ahead < 0, -band, band).astype(jnp.bfloat16)

    loads[0].wait()
    for h in range(nh):
        z = slice(h * SUB, (h + 1) * SUB)
        low = jnp.zeros((SUB, LANE), jnp.float32)
        high = low
        for f in range(fields):
            for i in range(nx):
                s = f * nx + i
                here = slot == s
                first, last = flow[f, i, z, :LANE], flow[f, i, z, ny - LANE:]
                low = jnp.where(here, pltpu.roll(first, 4 * s, 1) if s else first, low)
                high = jnp.where(here, pltpu.roll(last, (4 * s + 3) % LANE, 1), high)
        low = jnp.where(spot < 3, low, 0.0)
        high = jnp.where(spot < 3, high, 0.0)
        first = (
            (1.0 / 60.0) * low
            + jnp.where(spot >= 1, -9.0 / 60.0, 0.0) * pltpu.roll(low, 1, 1)
            + jnp.where(spot >= 2, 45.0 / 60.0, 0.0) * pltpu.roll(low, 2, 1)
        )
        last = (
            (-1.0 / 60.0) * high
            + jnp.where(spot < 2, 9.0 / 60.0, 0.0) * pltpu.roll(high, LANE - 1, 1)
            + jnp.where(spot < 1, -45.0 / 60.0, 0.0) * pltpu.roll(high, LANE - 2, 1)
        )
        first = jnp.where(spot < 3, first, 0.0)
        last = jnp.where(spot < 3, last, 0.0)
        halo_out[0, h] = first
        halo_out[1, h] = last
        edge_out[h * SUB:(h + 1) * SUB, 0, :] = first
        edge_out[nz + h * SUB:nz + (h + 1) * SUB, 0, :] = last

    @pl.when(owner)
    def _():
        pl.semaphore_wait(barrier, count - 1 + (1 + owners) * beside)

    @pl.when(jnp.logical_not(owner))
    def _():
        pl.semaphore_wait(barrier, owners + (1 + owners) * beside)

    halos = [
        pltpu.make_async_remote_copy(
            src_ref=halo_out.at[side],
            dst_ref=halo_in.at[side],
            send_sem=halo_send.at[side],
            recv_sem=halo_recv.at[side],
            device_id=(me, to),
            device_id_type=MESH,
        )
        for side, to in ((0, left), (1, right))
    ]
    def to_owners(act):
        for j in range(outer):
            to = lax.rem(block + j, outer)
            for r in reversed(range(deep)):
                act(j, to + outer * r, to * inner + (SHIFT + r) % inner)

    def edge_copy(side, across, w, device, p):
        return pltpu.make_async_remote_copy(
            src_ref=edge_out.at[pl.ds(side * nz + w * per + p, 1)],
            dst_ref=edge_in.at[pl.ds(((1 - side) * per + p) * count + me, 1)],
            send_sem=edge_send,
            recv_sem=edge_recv.at[section],
            device_id=(device, across),
            device_id_type=MESH,
        )

    def edge_span(parts, q):
        span = edge_in.at[pl.ds(0, parts * per)]
        return pltpu.make_async_remote_copy(
            src_ref=span, dst_ref=span, send_sem=edge_send, recv_sem=edge_recv.at[q],
            device_id=(me, wid), device_id_type=MESH,
        )

    def give_edges(j, w, device):
        for p in range(per):
            @pl.when(has_left)
            def _():
                edge_copy(0, left, w, device, p).start()

            @pl.when(has_right)
            def _():
                edge_copy(1, right, w, device, p).start()

    to_owners(give_edges)
    def each_halo(sent, got):
        for there, go, come in ((has_left, 0, 1), (has_right, 1, 0)):
            @pl.when(there)
            def _():
                if sent:
                    sent(halos[go])
                if got:
                    got(halos[come])

    each_halo(lambda halo: halo.start(), None)

    loads[4].wait()
    loads[3].wait()
    rows = nx * nz
    tiles = []
    for g in range(groups):
        one = ops[metric[g]]
        tiles.append(jnp.concatenate([one] * nx, axis=1))
    row_cell = lax.broadcasted_iota(jnp.int32, (nz, rows), 1) // nz
    diag = jnp.concatenate(
        [jnp.where(row_cell == i, tiles[i * groups // nx], 0.0) for i in range(nx)], axis=0
    )
    diag_high, diag_low = split_bf16(diag)

    loads[1].wait()
    for i in range(nx):
        c = cour[i]
        t = 1.0 / (1.0 + c)
        cour[i] = t
        k = jnp.where(c < 1.0, c * t, 1.0 - t)
        keep[i] = k
        gain[i] = STEP * t * flow[1, i]
        prod[i] = k if i == 0 else k * prod[i - 1]

    pulls = []
    after = None
    tiles = [jnp.zeros((SUB, LANE), jnp.float32) for _ in range(nh)]
    for i in reversed(range(nx)):
        weight = -gain[i] if after is None else -gain[i] * after
        after = keep[i] if after is None else after * keep[i]
        for h in range(nh):
            z = slice(h * SUB, (h + 1) * SUB)
            turned = pltpu.roll(weight[z, :LANE], 4 * i, 1) if i else weight[z, :LANE]
            tiles[h] = jnp.where(slot == i, turned, tiles[h])
            turned = pltpu.roll(weight[z, ny - LANE:], (4 * (nx + i) + 3) % LANE, 1)
            tiles[h] = jnp.where(slot == nx + i, turned, tiles[h])
    for h in range(nh):
        pulls.append(jnp.where(spot < 3, tiles[h], 0.0))
        send1[pl.ds(h * SUB * full + states, SUB, stride=full), 0, :] = pulls[h]
        for l in range(nl):
            send1[pl.ds(h * SUB * full + states + 1 + l, SUB, stride=full), 0, :] = prod[
                nx - 1, h * SUB:(h + 1) * SUB, l * LANE:(l + 1) * LANE
            ]

    def edge_terms(at_start, at_end, pull):
        lanes = lax.broadcasted_iota(jnp.int32, pull.shape, 1)

        def summed(edges, weights):
            spread = weights
            for f in range(1, fields):
                spread = spread + pltpu.roll(weights, f * field_lanes, 1)
            value = edges * spread
            step = field_lanes // 2
            while step >= 4:
                value = value + pltpu.roll(value, LANE - step, 1)
                step //= 2
            return value

        begin = summed(at_start, jnp.where(lanes < field_lanes, pull, 0.0))
        moved = pltpu.roll(pull, LANE - field_lanes, 1)
        end = summed(at_end, jnp.where(lanes < field_lanes, moved, 0.0))
        terms = []
        for f in range(fields):
            turned = pltpu.roll(begin, LANE - f * field_lanes, 1) if f else begin
            first = jnp.where(lanes < 3, turned, 0.0)
            turned = pltpu.roll(end, (2 * LANE - 3 - f * field_lanes) % LANE, 1)
            terms.append((first, jnp.where(lanes >= LANE - 3, turned, 0.0)))
        return terms

    loads[2].wait()
    height = lax.broadcasted_iota(jnp.int32, (nz, LANE), 0)
    starts = []
    for p in range(per):
        tile = jnp.zeros((SUB, LANE), jnp.float32)
        for f in range(fields):
            for l in range(nl):
                line = jnp.where(height == rank * per + p, infl[f, :, l * LANE:(l + 1) * LANE], 0.0)
                line = jnp.sum(line, axis=0, keepdims=True)
                tile = jnp.where(row == f * nl + l, jnp.broadcast_to(line, (SUB, LANE)), tile)
        starts.append(tile)

    for f in range(fields):
        q_high, q_low = split_bf16(flow[f].reshape(rows, ny))
        vertical = jnp.dot(diag_high, q_high, preferred_element_type=jnp.float32)
        vertical += jnp.dot(diag_low, q_high, preferred_element_type=jnp.float32)
        vertical += jnp.dot(diag_high, q_low, preferred_element_type=jnp.float32)
        slopes = jnp.dot(q_high, band, preferred_element_type=jnp.float32)
        slopes += jnp.dot(q_low, band, preferred_element_type=jnp.float32)
        for i in range(nx):
            at = slice(i * nz, (i + 1) * nz)
            tend = vertical[at] - flow[1, i] * ((1.0 / 60.0) * slopes[at])
            tend_ref[f, i] = tend
            new_ref[f, i] = cour[i] * (flow[f, i] + STEP * tend)

    def scatter(tile, v, h, l):
        send1[pl.ds(h * SUB * full + v * nl + l, SUB, stride=full), 0, :] = tile

    for h in range(nh):
        z = slice(h * SUB, (h + 1) * SUB)
        for l in range(nl):
            y = slice(l * LANE, (l + 1) * LANE)
            for f in range(fields):
                state = None
                for i in range(nx):
                    more = new_ref[f, i, z, y]
                    state = more if state is None else keep[i, z, y] * state + more
                    new_ref[f, i, z, y] = state
                scatter(state, f, h, l)

    def remote(source, target, phase, slot, device):
        return pltpu.make_async_remote_copy(
            src_ref=source,
            dst_ref=target,
            send_sem=ex_send.at[phase],
            recv_sem=ex_recv.at[slot],
            device_id=(device, wid),
            device_id_type=MESH,
        )

    def part(ref, k, size):
        return ref.at[pl.ds(k * size, size)]

    def total(ref, parts, phase, slot, size):
        span = ref.at[pl.ds(0, parts * size)]
        return remote(span, span, phase, slot, me)

    back = sections

    def give_map(j, w, device):
        def give():
            remote(part(send1, w, chunk), part(recv1, me, chunk), 0, section, device).start()

        if j:
            give()
        else:
            pl.when(me != device)(give)

    to_owners(give_map)

    each_halo(None, lambda halo: halo.wait_recv())
    for h in range(nh):
        z = slice(h * SUB, (h + 1) * SUB)
        fix_start = halo_in[1, h]
        fix_end = halo_in[0, h]
        for l in {0, nl - 1}:
            y = slice(l * LANE, (l + 1) * LANE)
            for f in range(fields):
                state = None
                for i in range(nx):
                    s = f * nx + i
                    fix = jnp.zeros((SUB, LANE), jnp.float32)
                    if l == 0:
                        turned = pltpu.roll(fix_start, LANE - 4 * s, 1) if s else fix_start
                        fix = jnp.where(lane < 3, turned, fix)
                    if l == nl - 1:
                        turned = pltpu.roll(fix_end, (2 * LANE - 3 - 4 * s) % LANE, 1)
                        fix = jnp.where(lane >= LANE - 3, turned, fix)
                    tend_ref[f, i, z, y] -= flow[1, i, z, y] * fix
                    more = gain[i, z, y] * fix
                    state = more if state is None else keep[i, z, y] * state + more
                    new_ref[f, i, z, y] -= state

    @pl.when(owner)
    def _():
        recv1[pl.ds(me * chunk, chunk)] = send1[pl.ds(rank * chunk, chunk)]
        entries = [start[:states] for start in starts]
        lines = lax.broadcasted_iota(jnp.int32, (states, LANE), 0)

        def send_back(q):
            for t in range(q * half, (q + 1) * half):
                def give():
                    remote(part(send3, t, back_rows), part(recv3, rank, back_rows), 1, back, t).start()

                if t in seats:
                    pl.when(me != t)(give)
                else:
                    give()

        for q in range(sections):
            @pl.when(section == q)
            def _():
                total(recv1, half - 1, 0, q, chunk).wait_recv()

            @pl.when(section != q)
            def _():
                total(recv1, half, 0, q, chunk).wait_recv()

            for sides in (1, 2):
                @pl.when(beside == sides)
                def _():
                    edge_span(sides * half, q).wait_recv()

            for p in range(per):
                at = p * count + q * half
                terms = edge_terms(
                    edge_in[at:at + half, 0, :],
                    edge_in[per * count + at:per * count + at + half, 0, :],
                    recv1[pl.ds(q * half * chunk + p * full + states, half, stride=chunk), 0, :],
                )
                for f in range(fields):
                    for l in range(nl):
                        term = jnp.zeros((half, LANE), jnp.float32)
                        if l == 0:
                            term += terms[f][0]
                        if l == nl - 1:
                            term += terms[f][1]
                        edge_tiles[pl.ds(at * SUB + f * nl + l, half, stride=SUB), :] = term

            for t in range(q * half, (q + 1) * half):
                for p in range(per):
                    at = t * back_rows + p * states
                    send3[at:at + states, 0, :] = entries[p]
                    decay = jnp.zeros((states, LANE), jnp.float32)
                    for l in range(nl):
                        line = recv1[t * chunk + p * full + states + 1 + l]
                        decay = jnp.where(lines % nl == l, jnp.broadcast_to(line, (states, LANE)), decay)
                    edge = edge_tiles[(p * count + t) * SUB:(p * count + t) * SUB + states, :]
                    entries[p] = decay * entries[p] + (recv1[t * chunk + p * full:t * chunk + p * full + states, 0, :] + edge)
            if q % 2 == 0:
                send_back(q)
                if q > 2:
                    send_back(q - 3)
        send_back(sections - 3)
        send_back(sections - 1)
        recv3[pl.ds(rank * back_rows, back_rows)] = send3[pl.ds(me * back_rows, back_rows)]
        total(recv3, owners - 1, 1, back, back_rows).wait_recv()

    @pl.when(jnp.logical_not(owner))
    def _():
        total(recv3, owners, 1, back, back_rows).wait_recv()

    for f in range(fields):
        for h in range(nh):
            for l in range(nl):
                enter = recv3[pl.ds(h * SUB * states + f * nl + l, SUB, stride=states), 0, :]
                z, y = slice(h * SUB, (h + 1) * SUB), slice(l * LANE, (l + 1) * LANE)
                for i in range(nx):
                    new_ref[f, i, z, y] += prod[i, z, y] * enter

    each_halo(lambda halo: halo.wait_send(), None)
    for sides in (1, 2):
        @pl.when(beside == sides)
        def _():
            edge_span(sides * owners, 0).wait_send()

    @pl.when(owner)
    def _():
        total(send1, owners - 1, 0, 0, chunk).wait_send()
        total(send3, count - 1, 1, back, back_rows).wait_send()

    @pl.when(jnp.logical_not(owner))
    def _():
        total(send1, owners, 0, 0, chunk).wait_send()


def store_kernel(new_in, tend_in, new_out, tend_out, sem):
    copies = [
        pltpu.make_async_copy(src, dst, sem.at[i])
        for i, (src, dst) in enumerate(((new_in, new_out), (tend_in, tend_out)))
    ]
    for copy in copies:
        copy.start()
    for copy in copies:
        copy.wait()


def shards(inner, deep, flow_state, courant, inflow, height_ops, metric_index):
    fields, nx, nz, ny = flow_state.shape
    count = lax.axis_size("len")
    nwid = lax.axis_size("wid")
    outer = count // inner
    owners = deep * outer
    full = (fields + 1) * (ny // LANE) + 1
    out = jax.ShapeDtypeStruct(flow_state.shape, jnp.float32)
    anywhere = pl.BlockSpec(memory_space=pl.ANY)
    nh = nz // SUB
    states = fields * (ny // LANE)
    heights = nz // owners * count
    f32 = jnp.float32
    dma = pltpu.SemaphoreType.DMA
    held = [
        pltpu.with_memory_space_constraint(value, pltpu.HBM)
        for value in (flow_state, courant, inflow, height_ops, metric_index)
    ]
    new_state, tendency = pl.pallas_call(
        functools.partial(sweep_kernel, inner, outer, deep, nwid, metric_index.shape[0]),
        out_shape=(out, out),
        in_specs=[pl.BlockSpec(memory_space=pltpu.HBM)] * 5,
        out_specs=(pl.BlockSpec(memory_space=pltpu.VMEM),) * 2,
        scratch_shapes=[
            pltpu.VMEM(flow_state.shape, f32),
            pltpu.VMEM(courant.shape, f32),
            pltpu.VMEM(inflow.shape, f32),
            pltpu.VMEM(height_ops.shape, f32),
            pltpu.SMEM(metric_index.shape, jnp.int32),
            pltpu.VMEM(courant.shape, f32),
            pltpu.VMEM(courant.shape, f32),
            pltpu.VMEM(courant.shape, f32),
            pltpu.VMEM((2, nh, SUB, LANE), f32),
            pltpu.VMEM((2, nh, SUB, LANE), f32),
            pltpu.VMEM((2 * nz, 1, LANE), f32),
            pltpu.VMEM((2 * heights, 1, LANE), f32),
            pltpu.VMEM((heights * SUB, LANE), f32),
            pltpu.VMEM((nz * full, 1, LANE), f32),
            pltpu.VMEM((heights * full, 1, LANE), f32),
            pltpu.VMEM((heights * states, 1, LANE), f32),
            pltpu.VMEM((nz * states, 1, LANE), f32),
            dma((5,)),
            dma((2,)),
            dma((2,)),
            dma,
            dma((2 * outer,)),
            dma((2,)),
            dma((2 * outer + 1,)),
        ],
        compiler_params=pltpu.CompilerParams(
            collective_id=0, has_side_effects=True, vmem_limit_bytes=16 << 20
        ),
        name="sweep",
    )(*held)
    return pl.pallas_call(
        store_kernel,
        out_shape=(out, out),
        in_specs=[anywhere] * 2,
        out_specs=(anywhere, anywhere),
        scratch_shapes=[dma((2,))],
        compiler_params=pltpu.CompilerParams(vmem_limit_bytes=4 << 20),
        name="finish",
    )(new_state, tendency)


def solution(mesh, inner=16, deep=4):
    placed = (
        P(None, "len", None, "wid"),
        P("len", None, "wid"),
        P(None, None, "wid"),
        P(),
        P("len"),
    )
    return jax.shard_map(
        functools.partial(shards, inner, deep),
        mesh=mesh,
        in_specs=placed,
        out_specs=(P(None, "len", None, "wid"), P(None, "len", None, "wid")),
        check_vma=False,
    )
```
